128 devices in a mesh: leaf: 8 (over x, core), prow: 4 (over z), pcol: 4 (over y).
Axes of the slice: x: 4, y: 4, z: 4, core: 2. Of those that a mesh axis runs over, the one named last changes fastest.
Arguments:
- subtree_factor: float32 [8, 2, 8, 256, 2048], P('leaf', None, None, 'prow', 'pcol'), may hold values from -0.09375 to 0.09375
- sub_linv: float32 [8, 2, 8, 256, 256], P('leaf', None, None, 'prow'), may hold values from -0.05 to 1.05
- sub_uinv: float32 [8, 2, 8, 256, 256], P('leaf', None, None, 'prow'), may hold values from -0.05 to 1.05
- lower_panel: float32 [8, 4, 256, 2, 2048], P('leaf', None, 'prow', None, 'pcol'), may hold values from -0.0234375 to 0.0234375
- upper_panel: float32 [8, 2, 8, 256, 1024], P('leaf', None, None, 'prow', 'pcol'), may hold values from -0.125 to 0.125
- panel_rows: int32 [8, 4, 2], P('leaf'), may hold values 0 or 1
- upper_level_factor: float32 [4, 256, 1024], P(None, 'prow', 'pcol'), may hold values from -0.125 to 0.125
- top_linv: float32 [4, 256, 256], P(None, 'prow'), may hold values from -0.05 to 1.05
- top_uinv: float32 [4, 256, 256], P(None, 'prow'), may hold values from -0.05 to 1.05
- sub_rhs: float32 [8, 2, 8, 256, 256], P('leaf', None, None, 'prow'), may hold values from -6 to 6
- top_rhs: float32 [4, 256, 256], P(None, 'prow', 'leaf'), may hold values from -6 to 6
Outputs:
- sub_solution: float32 [8, 2, 8, 256, 256], P('leaf', None, 'pcol')
- top_solution: float32 [4, 256, 256], P('pcol', None, 'leaf')
The draws below stay inside these ranges and needn't reach their ends.
All inputs are finite; a program needn't handle non-finite values. No bound on the sum of `panel_rows` on one device may be relied on, other than what follows from the above.
Results may differ from the reference program's by a relative error of at most 0.00013.
Values sent between devices are 32-bit elements; how exact they have to be, the bound alone decides.
A program may use at most 128 MiB of HBM per device.

```python
import jax
import jax.numpy as jnp
from jax import lax

NB = 256
NR = 256
SUB = 2
NS = 8
NT = 4
LAYERS = 8


def near_identity(key, leading):
    spread = jax.random.uniform(key, leading + (NB, NB), jnp.float32, -0.05, 0.05)
    return spread + jnp.eye(NB, dtype=jnp.float32)


def draw_sub_linv(key, part):
    return near_identity(jax.random.fold_in(key, 11), (LAYERS, SUB, NS))


def draw_sub_uinv(key, part):
    return near_identity(jax.random.fold_in(key, 23), (LAYERS, SUB, NS))


def draw_top_linv(key, part):
    return near_identity(jax.random.fold_in(key, 37), (NT,))


def draw_top_uinv(key, part):
    return near_identity(jax.random.fold_in(key, 41), (NT,))


def touch_ends(values, stream_key, least, high):
    longest = values.shape.index(max(values.shape))
    spots = []
    for shift in (0, 1):
        where = [jax.random.randint(jax.random.fold_in(stream_key, axis), (), 0, length) for axis, length in enumerate(values.shape)]
        where[longest] = (where[longest] + shift) % values.shape[longest]
        spots.append(tuple(where))
    return values.at[spots[0]].set(least).at[spots[1]].set(high)


def shard_levels(rng, extent, shards, least, top_value):
    def one(position, parts):
        heights = jax.random.uniform(jax.random.fold_in(jax.random.fold_in(rng, 6), position), (parts,), jnp.float32, least / len(shards), top_value / len(shards))
        return jnp.repeat(jnp.exp(heights), extent[position] // parts).reshape((-1,) + (1,) * (len(extent) - position - 1))

    loudness = one(*shards[0])
    for cut in shards[1:]:
        loudness = loudness * one(*cut)
    return loudness


def gaussian(stream_key, extent, scale, bound, cuts=(), held_as=jnp.bfloat16):
    entries = scale * jax.random.normal(stream_key, extent, jnp.float32)
    if cuts:
        entries = entries * shard_levels(stream_key, extent, cuts, -0.22, 0.18)
    return jnp.clip(entries, -bound, bound).astype(held_as)


def setup_inputs(seed: int = 0) -> dict:
    key_list = jax.random.split(jax.random.key(seed), 12)
    return {
        "subtree_factor": gaussian(key_list[0], (LAYERS, SUB, NS, NB, NS * NB), (2 * NS * NB) ** -0.5, 0.09375, ((0, 8), (3, 4), (4, 4)), jnp.float32),
        "sub_linv": draw_sub_linv(jax.random.fold_in(key_list[11], 71), 0),
        "sub_uinv": draw_sub_uinv(jax.random.fold_in(key_list[11], 71), 0),
        "lower_panel": gaussian(key_list[3], (LAYERS, NT, NB, SUB, NS * NB), (2 * LAYERS * SUB * NS * NB) ** -0.5, 0.0234375, ((0, 8), (2, 4), (4, 4)), jnp.float32),
        "upper_panel": gaussian(key_list[4], (LAYERS, SUB, NS, NB, NT * NB), (2 * NT * NB) ** -0.5, 0.125, ((0, 8), (3, 4), (4, 4)), jnp.float32),
        "panel_rows": touch_ends((jax.random.randint(key_list[5], (LAYERS, NT, SUB), 0, 3) < 2).astype(jnp.int32), jax.random.fold_in(key_list[5], 1), 0, 1),
        "upper_level_factor": gaussian(key_list[6], (NT, NB, NT * NB), (2 * NT * NB) ** -0.5, 0.125, ((1, 4), (2, 4)), jnp.float32),
        "top_linv": draw_top_linv(jax.random.fold_in(key_list[11], 71), 0),
        "top_uinv": draw_top_uinv(jax.random.fold_in(key_list[11], 71), 0),
        "sub_rhs": gaussian(key_list[9], (LAYERS, SUB, NS, NB, NR), 1.0, 6.0, ((0, 8), (3, 4)), jnp.float32),
        "top_rhs": gaussian(key_list[10], (NT, NB, NR), 1.0, 6.0, ((1, 4), (2, 8)), jnp.float32),
    }


TOP_PRECISION = lax.Precision.HIGHEST


def solve_chain(blocks, inverses, right_side, coupling, forward):
    block_count = blocks.shape[2]
    solved = jnp.zeros(right_side.shape, jnp.float32)
    order_list = range(block_count) if forward else range(block_count - 1, -1, -1)
    for sweep_step_index in order_list:
        first_block, last_block = (0, sweep_step_index) if forward else (sweep_step_index + 1, block_count)
        partial_value = coupling[:, :, sweep_step_index]
        if last_block > first_block:
            partial_value = partial_value + jnp.einsum('jsakb,jskbr->jsar', blocks[:, :, sweep_step_index, :, first_block:last_block], solved[:, :, first_block:last_block], precision=TOP_PRECISION)
        block_value = jnp.einsum('jsab,jsar->jsbr', inverses[:, :, sweep_step_index], right_side[:, :, sweep_step_index] - partial_value, precision=TOP_PRECISION)
        solved = solved.at[:, :, sweep_step_index].set(block_value)
    return solved


def reference(subtree_factor, sub_linv, sub_uinv, lower_panel, upper_panel, panel_rows, upper_level_factor, top_linv, top_uinv, sub_rhs, top_rhs):
    layers, groups, block_count, block_rows, columns = sub_rhs.shape
    top_count = top_rhs.shape[0]
    sub_blocks = subtree_factor.reshape(layers, groups, block_count, block_rows, block_count, block_rows)
    top_blocks = upper_level_factor.reshape(1, 1, top_count, block_rows, top_count, block_rows)
    present = panel_rows.astype(jnp.float32)
    lower_sub = solve_chain(sub_blocks, sub_linv, sub_rhs, jnp.zeros(sub_rhs.shape, jnp.float32), True)

    def add_layer(carried, pieces):
        panel_piece, mask_piece, solved_piece = pieces
        flat_solved = solved_piece.reshape(groups, block_count * block_rows, columns)
        layer_term = jnp.einsum('tasm,ts,smr->tar', panel_piece, mask_piece, flat_solved, precision=TOP_PRECISION)
        return carried + layer_term, None

    contrib, ignored = lax.scan(add_layer, jnp.zeros(top_rhs.shape, jnp.float32), (lower_panel, present, lower_sub))
    upper_level_lower = solve_chain(top_blocks, top_linv[None, None], top_rhs[None, None], contrib[None, None], True)
    top_solution = solve_chain(top_blocks, top_uinv[None, None], upper_level_lower, jnp.zeros(upper_level_lower.shape, jnp.float32), False)[0, 0]
    upper_blocks = upper_panel.reshape(layers, groups, block_count, block_rows, top_count, block_rows)
    coupling = jnp.einsum('jskatb,jts,tbr->jskar', upper_blocks, present, top_solution, precision=TOP_PRECISION)
    sub_solution = solve_chain(sub_blocks, sub_uinv, lower_sub, coupling, False)
    return sub_solution, top_solution
```

```python
import jax
import jax.numpy as jnp
from jax import lax
from jax.experimental import pallas as pl
from jax.experimental.pallas import tpu as pltpu
from jax.sharding import PartitionSpec as P

MESH = pl.DeviceIdType.MESH
F32 = jnp.float32
BF16 = jnp.bfloat16
NPOS = 18
SEND_AT = {-1: (0, 1, 2), 0: (3,), 1: (4,), 2: (5,), 3: (6, 7), 4: (8,), 5: (9,), 6: (10,), 7: (11, 12), 8: (13,), 9: (14,), 10: (15,), 11: (16,), 12: (17,)}
RELAY_AT = {0: (0, 1), 1: (2,), 2: (3,), 3: (4,), 4: (5,), 5: (6, 7), 6: (8,), 7: (9, 10), 8: (11, 12), 9: (13,), 10: (14,), 11: (15,), 12: (16,), 13: (17,)}
ARRIVE_AT = {0: (0,), 1: (1,), 2: (2,), 3: (3,), 4: (4,), 5: (5,), 6: (6,), 7: (7, 8), 8: (11, 12), 10: (13,), 11: (14,), 12: (15,), 13: (16,), 14: (17,)}


def halves(value):
    high = value.astype(BF16)
    return high, (value - high.astype(F32)).astype(BF16)


def product(left, right):
    def one(a, b):
        return jnp.dot(a, b, preferred_element_type=F32)

    return one(left[0], right[0]) + (one(left[0], right[1]) + one(left[1], right[0]))


def kernel(
    present_ref,
    factor,
    linv,
    uinv,
    lower,
    upper,
    topf,
    tlinv,
    tuinv,
    rhs,
    toprhs,
    sub_out,
    top_out,
    slab,
    lowers,
    uppers,
    tops,
    inv,
    base,
    gath,
    sol,
    solh,
    soll,
    invh,
    invl,
    coup,
    part,
    red,
    trhs,
    swap,
    ssem_y,
    rsem_y,
    ssem_i,
    rsem_i,
    ssem_g,
    rsem_g,
    ssem_r,
    rsem_r,
    ssem_a,
    rsem_a,
    ssem_o,
    rsem_o,
    misc,
    ssem_x,
    rsem_x,
):
    leaf = lax.axis_index("leaf")
    row = lax.axis_index("prow")
    col = lax.axis_index("pcol")
    sub = col // 2
    half = lax.rem(col + sub, 2)
    beside = col + 1 - 2 * lax.rem(col, 2)
    across = 3 - col
    rows = pl.ds(pl.multiple_of(row * 64, 64), 64)

    def zpeer(d):
        return (leaf, lax.rem(row + d, 4), col)

    def ypeer(c):
        return (leaf, row, c)

    group = []
    for other in (0, 1):
        for d in range(8):
            if other or d:
                group.append((other, d))

    def member(other, d):
        there = lax.rem(leaf + d, 8)
        return (there, row, across if other else col), (1 - sub if other else sub) * 8 + there

    barrier = pltpu.get_barrier_semaphore()
    greeted = [zpeer(d) for d in (1, 2, 3)]
    greeted += [ypeer(beside), ypeer(3 - beside)]
    greeted += [member(o, d)[0] for o, d in group]
    for peer in greeted:
        pl.semaphore_signal(barrier, inc=1, device_id=peer, device_id_type=MESH)
    pl.semaphore_wait(barrier, len(greeted))

    def remote(src, dst, send, recv, peer):
        return pltpu.make_async_remote_copy(
            src_ref=src, dst_ref=dst, send_sem=send, recv_sem=recv, device_id=peer, device_id_type=MESH
        )

    def arrived(ref, sem):
        pltpu.make_async_copy(ref, ref, sem).wait()

    def piece(owner, p):
        near = 7 - 2 * owner
        if p < near:
            i = 2 * owner + 1 + p
            if p == 0:
                return lambda s: factor.at[s, i, :, pl.ds(0, 256)], slab.at[owner, i, :, pl.ds(0, 256)]
            return lambda s: factor.at[s, i], slab.at[owner, i]
        if p < near + 4:
            t = p - near
            return lambda s: lower.at[s, t], lowers.at[owner, t]
        if p < near + 6:
            t = pl.ds(2 * (p - near - 4), 2)
            return lambda s: topf.at[t], tops.at[owner, t]
        if p < near + 10:
            i = pl.ds(2 * (p - near - 6), 2)
            return lambda s: upper.at[s, i], uppers.at[owner, i]
        i = 2 * owner - (p - near - 10)
        return lambda s: factor.at[s, i], slab.at[owner, i]

    def travel(sends=(), relays=(), arrivals=(), first=False, last=False):
        for o in range(4):
            mine, there, over = o // 2, 1 - o // 2, 3 - o

            @pl.when(col == o)
            def _():
                if first:
                    for p in range(NPOS):
                        src, dst = piece(o, p)
                        pltpu.make_async_copy(src(mine), dst, rsem_y.at[p, o]).start()
                for p in sends:
                    src, dst = piece(o, p)
                    remote(src(mine), dst, ssem_y.at[p, 0], rsem_y.at[p, o], ypeer(o ^ 1)).start()
                    remote(src(there), dst, ssem_y.at[p, 1], rsem_y.at[p, o], ypeer(over)).start()
                for p in relays:
                    dst = piece(over, p)[1]
                    arrived(dst, rsem_y.at[p, over])
                    remote(dst, dst, ssem_y.at[p, 2], rsem_y.at[p, over], ypeer(o ^ 1)).start()
                for p in arrivals:
                    for other in (o, o ^ 1, 3 - (o ^ 1)):
                        arrived(piece(other, p)[1], rsem_y.at[p, other])
                if last:
                    for p in range(NPOS):
                        dst = piece(o, p)[1]
                        arrived(dst, ssem_y.at[p, 0])
                        arrived(dst, ssem_y.at[p, 1])
                        arrived(piece(over, p)[1], ssem_y.at[p, 2])

    def inverse_of(n):
        if n < 8:
            return linv.at[sub, n]
        if n < 12:
            return tlinv.at[n - 8]
        if n < 16:
            return tuinv.at[15 - n]
        return uinv.at[sub, 23 - n]

    def send_inverse(n):
        for d in (1, 2, 3):
            remote(inverse_of(n), inv.at[n, row], ssem_i.at[n, d - 1], rsem_i.at[n, d], zpeer(d)).start()
        pltpu.make_async_copy(inverse_of(n), inv.at[n, row], rsem_i.at[n, 0]).start()

    def prepare_inverse(n):
        for d in range(4):
            arrived(inv.at[0, 0], rsem_i.at[n, d])
        whole = inv[n].reshape(256, 256).T
        invh[n % 2], invl[n % 2] = halves(whole)

    def sub_block(i, k):
        return slab[k // 2, i, :, (k % 2) * 256 : (k % 2) * 256 + 256]

    def terms(n):
        if n < 8:
            return [(lambda k=k: sub_block(n, k), k) for k in range(n)]
        if n < 12:
            return [(lambda u=u: tops[u, n - 8], 8 + u) for u in range(n - 8)]
        if n < 16:
            t = 15 - n
            return [(lambda u=u: tops[u, t], 15 - u) for u in range(3, t, -1)]
        i = 23 - n
        return [(lambda k=k: sub_block(i, k), 23 - k) for k in range(7, i, -1)]

    def apply(block, n):
        return product(halves(block()), (solh[n], soll[n]))

    def base_of(n):
        if n < 8:
            return base[n]
        if n < 12:
            return trhs[pl.ds((n - 8) * 4, 4)].reshape(64, 128)
        if n < 16:
            return sol[23 - n, rows]
        return sol[23 - n, rows] - coup[23 - n]

    def before(n):
        value = base_of(n)
        for block, k in terms(n):
            if k != n - 1:
                value = value - apply(block, k)
        return value

    def finish(n, value):
        for block, k in terms(n):
            if k == n - 1:
                value = value - apply(block, k)
        return value

    def start_gather(n, value):
        gath[n, rows] = value
        for d in (1, 2, 3):
            remote(gath.at[n, rows], gath.at[n, rows], ssem_g.at[n, d - 1], rsem_g.at[n, d - 1], zpeer(d)).start()

    def solve(n):
        for d in (1, 2, 3):
            arrived(gath.at[0, pl.ds(0, 64)], rsem_g.at[n, d - 1])
        value = product((invh[n % 2], invl[n % 2]), halves(gath[n]))
        sol[n] = value
        solh[n], soll[n] = halves(value)

    def mask(t):
        return present_ref[t, sub].astype(F32)

    def contrib(owner):
        pair = (
            jnp.concatenate([solh[2 * owner], solh[2 * owner + 1]], axis=0),
            jnp.concatenate([soll[2 * owner], soll[2 * owner + 1]], axis=0),
        )
        for t in range(4):
            value = product(halves(lowers[owner, t]), pair) * mask(t)
            part[pl.ds(4 * t, 4)] += value.reshape(4, 16, 128)

    def couple(t, first, last):
        value = product(halves(uppers[t, first:last].reshape((last - first) * 64, 256)), (solh[15 - t], soll[15 - t]))
        return (value * mask(t)).reshape(last - first, 64, 128)

    base_copy = pltpu.make_async_copy(
        rhs.at[sub, :, :, pl.ds(pl.multiple_of(half * 128, 128), 128)], base, misc.at[0]
    )
    base_copy.start()
    send_inverse(0)
    travel(first=True, sends=SEND_AT[-1])
    send_inverse(1)
    quarter = lax.broadcasted_iota(jnp.int32, (256, 128), 1) // 32
    narrow = toprhs[...].reshape(256, 32)
    spread = jnp.concatenate([narrow] * 4, axis=1)
    here = jnp.where(jnp.logical_and(leaf // 4 == half, sub == 0), lax.rem(leaf, 4), -1)
    part[...] = -jnp.where(quarter == here, spread, 0.0).reshape(16, 16, 128)
    base_copy.wait()
    carried = base_of(0)

    for n in range(24):
        if n == 8:
            contrib(3)
            travel(arrivals=(9, 10))
            contrib(0)
            me = sub * 8 + leaf
            red[pl.ds(me, 1)] = part[pl.ds(me, 1)]
            for k, (o, d) in enumerate(group):
                peer, m = member(o, d)
                remote(part.at[m], red.at[me], ssem_r.at[k], rsem_r.at[k], peer).start()
            for k in range(15):
                arrived(red.at[0], rsem_r.at[k])
            total = red[0]
            for m in range(1, 16):
                total = total + red[m]
            trhs[pl.ds(me, 1)] = -total[None]
            for k, (o, d) in enumerate(group):
                peer, m = member(o, d)
                remote(trhs.at[me], trhs.at[me], ssem_a.at[k], rsem_a.at[k], peer).start()
            for k in range(15):
                arrived(trhs.at[0], rsem_a.at[k])
            carried = base_of(8)
        if n == 12:
            value = sol[11, rows]
        elif n == 16:
            value = sol[7, rows] - coup[7] - couple(0, 7, 8)[0]
        else:
            value = finish(n, carried)
        start_gather(n, value)
        if n + 2 < 24:
            send_inverse(n + 2)
        travel(sends=SEND_AT.get(n, ()), relays=RELAY_AT.get(n, ()))
        prepare_inverse(n)
        travel(arrivals=ARRIVE_AT.get(n, ()))
        if n == 7:
            contrib(2)
        if n == 16:
            coup[0:7] += couple(0, 0, 7)
            for o in range(4):

                @pl.when(col == o)
                def _():
                    remote(sol.at[15 - (o ^ 1)], swap, ssem_x.at[0], rsem_x.at[0], ypeer(o ^ 1)).start()

        if n == 14:
            coup[...] = couple(3, 0, 8) + couple(2, 0, 8)
        if n == 15:
            coup[...] += couple(1, 0, 8)
        if n + 1 not in (8, 12, 16, 24):
            carried = before(n + 1)
        if n == 7:
            contrib(1)
        solve(n)
        if n >= 16:
            i = 23 - n
            o = i // 2
            place = sub_out.at[0, sub, i % 2, :, pl.ds(pl.multiple_of(half * 128, 128), 128)]

            @pl.when(col == o)
            def _():
                pltpu.make_async_copy(sol.at[n], place, rsem_o.at[i % 2, col]).start()

            @pl.when(col != o)
            def _():
                remote(sol.at[n], place, ssem_o.at[i], rsem_o.at[i % 2, col], ypeer(o)).start()

    arrived(swap, rsem_x.at[0])
    top = jnp.where(leaf // 4 == half, sol[15 - col], swap[...])
    q = lax.rem(leaf, 4)
    picked = top[:, 0:32]
    for k in range(1, 4):
        picked = jnp.where(q == k, top[:, 32 * k : 32 * k + 32], picked)
    top_out[0] = picked

    travel(last=True)
    for n in range(24):
        for d in range(3):
            arrived(inv.at[0, 0], ssem_i.at[n, d])
            arrived(gath.at[0, pl.ds(0, 64)], ssem_g.at[n, d])
    for k in range(15):
        arrived(red.at[0], ssem_r.at[k])
        arrived(red.at[0], ssem_a.at[k])
    arrived(swap, ssem_x.at[0])
    for i in range(8):

        @pl.when(col != i // 2)
        def _():
            arrived(sol.at[0], ssem_o.at[i])

    for k in range(2):
        for c in range(4):
            arrived(sol.at[0], rsem_o.at[k, c])


def per_device(
    subtree_factor, sub_linv, sub_uinv, lower_panel, upper_panel, panel_rows, upper_level_factor, top_linv, top_uinv, sub_rhs, top_rhs
):
    anywhere = pl.BlockSpec(memory_space=pl.ANY)
    vmem = pl.BlockSpec(memory_space=pltpu.VMEM)
    dma = pltpu.SemaphoreType.DMA
    return pl.pallas_call(
        kernel,
        name="solve",
        out_shape=(
            jax.ShapeDtypeStruct((1, 2, 2, 256, 256), F32),
            jax.ShapeDtypeStruct((1, 256, 32), F32),
        ),
        in_specs=[pl.BlockSpec(memory_space=pltpu.SMEM)] + [anywhere] * 9 + [vmem],
        out_specs=(anywhere, vmem),
        scratch_shapes=[
            pltpu.VMEM((4, 8, 64, 512), F32),
            pltpu.VMEM((4, 4, 64, 512), F32),
            pltpu.VMEM((4, 8, 64, 256), F32),
            pltpu.VMEM((4, 4, 64, 256), F32),
            pltpu.VMEM((24, 4, 64, 256), F32),
            pltpu.VMEM((8, 64, 128), F32),
            pltpu.VMEM((24, 256, 128), F32),
            pltpu.VMEM((24, 256, 128), F32),
            pltpu.VMEM((24, 256, 128), BF16),
            pltpu.VMEM((24, 256, 128), BF16),
            pltpu.VMEM((2, 256, 256), BF16),
            pltpu.VMEM((2, 256, 256), BF16),
            pltpu.VMEM((8, 64, 128), F32),
            pltpu.VMEM((16, 16, 128), F32),
            pltpu.VMEM((16, 16, 128), F32),
            pltpu.VMEM((16, 16, 128), F32),
            pltpu.VMEM((256, 128), F32),
            dma((NPOS, 3)),
            dma((NPOS, 4)),
            dma((24, 3)),
            dma((24, 4)),
            dma((24, 3)),
            dma((24, 3)),
            dma((15,)),
            dma((15,)),
            dma((15,)),
            dma((15,)),
            dma((8,)),
            dma((2, 4)),
            dma((1,)),
            dma((1,)),
            dma((1,)),
        ],
        compiler_params=pltpu.CompilerParams(collective_id=0, has_side_effects=True, vmem_limit_bytes=56 << 20),
    )(
        panel_rows[0],
        subtree_factor[0],
        sub_linv[0],
        sub_uinv[0],
        jnp.transpose(lower_panel[0], (2, 0, 1, 3)),
        upper_panel[0],
        upper_level_factor,
        top_linv,
        top_uinv,
        sub_rhs[0],
        top_rhs,
    )


def solution(mesh):
    placed = (
        P("leaf", None, None, "prow", "pcol"),
        P("leaf", None, None, "prow", None),
        P("leaf", None, None, "prow", None),
        P("leaf", None, "prow", None, "pcol"),
        P("leaf", None, None, "prow", "pcol"),
        P("leaf", None, None),
        P(None, "prow", "pcol"),
        P(None, "prow", None),
        P(None, "prow", None),
        P("leaf", None, None, "prow", None),
        P(None, "prow", "leaf"),
    )
    return jax.shard_map(
        per_device,
        mesh=mesh,
        in_specs=placed,
        out_specs=(P("leaf", None, "pcol", None, None), P("pcol", None, "leaf")),
        check_vma=False,
    )
```

```python
import jax
import jax.numpy as jnp
from jax import lax
from jax.experimental import pallas as pl
from jax.experimental.pallas import tpu as pltpu
from jax.sharding import PartitionSpec as P

MESH = pl.DeviceIdType.MESH
F32 = jnp.float32
BF16 = jnp.bfloat16
NPOS = 22
SEND_AT = {-1: (0, 1, 2), 0: (3,), 1: (4,), 2: (5,), 3: (6,), 4: (7, 8), 5: (9,), 6: (10,), 7: (11,), "sum": (12,), "share": (13, 14), 8: (16,), 9: (17,), 10: (18,), 11: (19,), 12: (20,), 13: (21,), "top": (15,)}
RELAY_AT = {0: (0, 1), 1: (2,), 2: (3,), 3: (4,), 4: (5,), 5: (6, 7), 6: (8,), 7: (9, 10), "share": (11, 12), "top": (13, 14), 8: (15,), 9: (16,), 10: (17,), 11: (18,), 12: (19,), 13: (20,), 14: (21,)}
ARRIVE_AT = {0: (0,), 1: (1,), 2: (2,), 3: (3,), 4: (4,), 5: (5,), 6: (6,), 7: (7, 8), "end": (9, 10), "top": (11, 12, 13, 14), 8: (15,), 9: (16,), 10: (17,), 11: (18,), 12: (19,), 13: (20,), 14: (21,)}


def halves(value):
    high = value.astype(BF16)
    return high, (value - high.astype(F32)).astype(BF16)


def product(left, right):
    def one(a, b):
        return jnp.dot(a, b, preferred_element_type=F32)

    return one(left[0], right[0]) + (one(left[0], right[1]) + one(left[1], right[0]))


def kernel(
    present_ref,
    factor,
    linv,
    uinv,
    lower,
    upper,
    topf,
    tlinv,
    tuinv,
    rhs,
    toprhs,
    sub_out,
    top_out,
    slab,
    lowers,
    uppers,
    tops,
    inv,
    base,
    gath,
    sol,
    solh,
    soll,
    invh,
    invl,
    coup,
    part,
    red,
    trhs,
    swap,
    blockh,
    blockl,
    tsol,
    tsolh,
    tsoll,
    ssem_y,
    rsem_y,
    ssem_i,
    rsem_i,
    ssem_g,
    rsem_g,
    ssem_r,
    rsem_r,
    ssem_a,
    rsem_a,
    ssem_o,
    rsem_o,
    misc,
    ssem_x,
    rsem_x,
    ssem_t,
    rsem_t,
    ssem_v,
    rsem_v,
    ssem_w,
    rsem_w,
    ssem_p,
    rsem_p,
    ssem_q,
    rsem_q,
):
    leaf = lax.axis_index("leaf")
    row = lax.axis_index("prow")
    col = lax.axis_index("pcol")
    sub = col // 2
    half = lax.rem(col + sub, 2)
    beside = col + 1 - 2 * lax.rem(col, 2)
    across = 3 - col
    rows = pl.ds(pl.multiple_of(row * 64, 64), 64)

    def zpeer(d):
        return (leaf, lax.rem(row + d, 4), col)

    def ypeer(c):
        return (leaf, row, c)

    group = []
    for other in (0, 1):
        for d in range(8):
            if other or d:
                group.append((other, d))

    def member(other, d):
        there = lax.rem(leaf + d, 8)
        return (there, row, across if other else col), (1 - sub if other else sub) * 8 + there

    core = lax.rem(leaf, 2)
    mine_t = leaf // 2
    partner = (leaf + 1 - 2 * core, row, col)
    wide = []
    for other in (0, 1):
        for dx in range(4):
            for dr in range(4):
                if other or dx or dr:
                    wide.append((lax.rem(leaf + 2 * dx, 8), lax.rem(row + dr, 4), across if other else col))

    def xpeer(d):
        return (lax.rem(leaf + 2 * d, 8), row, col)

    barrier = pltpu.get_barrier_semaphore()
    greeted = wide + [ypeer(beside), ypeer(3 - beside)]
    greeted += [member(o, d)[0] for o, d in group if d % 2]
    for peer in greeted:
        pl.semaphore_signal(barrier, inc=1, device_id=peer, device_id_type=MESH)
    pl.semaphore_wait(barrier, len(greeted))

    def remote(src, dst, send, recv, peer):
        return pltpu.make_async_remote_copy(
            src_ref=src, dst_ref=dst, send_sem=send, recv_sem=recv, device_id=peer, device_id_type=MESH
        )

    def arrived(ref, sem):
        pltpu.make_async_copy(ref, ref, sem).wait()

    def piece(owner, p):
        near = 7 - 2 * owner
        if p < near:
            i = 2 * owner + 1 + p
            if p == 0:
                return lambda s: factor.at[s, i, :, pl.ds(0, 256)], slab.at[owner, i, :, pl.ds(0, 256)]
            return lambda s: factor.at[s, i], slab.at[owner, i]
        if p < near + 4:
            t = p - near
            return lambda s: lower.at[t, :, s], lowers.at[owner, t]
        if p < 11:
            return None
        if p < 15:
            i = pl.ds(2 * (p - 11), 2)
            return lambda s: upper.at[s, i], uppers.at[owner, i]
        i = 21 - p
        if i > 2 * owner:
            return None
        if i == 2 * owner:
            return lambda s: factor.at[s, i, :, pl.ds(256, 256)], slab.at[owner, i, :, pl.ds(256, 256)]
        return lambda s: factor.at[s, i], slab.at[owner, i]

    def travel(sends=(), relays=(), arrivals=(), first=False, last=False):
        for o in range(4):
            mine, there, over = o // 2, 1 - o // 2, 3 - o

            @pl.when(col == o)
            def _():
                if first:
                    for p in range(NPOS):
                        if piece(o, p):
                            src, dst = piece(o, p)
                            pltpu.make_async_copy(src(mine), dst, rsem_y.at[p, o]).start()
                for p in sends:
                    if piece(o, p):
                        src, dst = piece(o, p)
                        remote(src(mine), dst, ssem_y.at[p, 0], rsem_y.at[p, o], ypeer(o ^ 1)).start()
                        remote(src(there), dst, ssem_y.at[p, 1], rsem_y.at[p, o], ypeer(over)).start()
                for p in relays:
                    if piece(over, p):
                        dst = piece(over, p)[1]
                        arrived(dst, rsem_y.at[p, over])
                        remote(dst, dst, ssem_y.at[p, 2], rsem_y.at[p, over], ypeer(o ^ 1)).start()
                for p in arrivals:
                    for other in (o, o ^ 1, 3 - (o ^ 1)):
                        if piece(other, p):
                            arrived(piece(other, p)[1], rsem_y.at[p, other])
                if last:
                    for p in range(NPOS):
                        if piece(o, p):
                            dst = piece(o, p)[1]
                            arrived(dst, ssem_y.at[p, 0])
                            arrived(dst, ssem_y.at[p, 1])
                        if piece(over, p):
                            arrived(piece(over, p)[1], ssem_y.at[p, 2])

    def at(point):
        travel(SEND_AT.get(point, ()), RELAY_AT.get(point, ()), ARRIVE_AT.get(point, ()))

    my_rows = pl.ds(pl.multiple_of(core * 32, 32), 32)

    def collect_top():
        for d in (1, 2, 3):
            remote(topf.at[mine_t, my_rows], tops.at[mine_t, core, col, row], ssem_t.at[d - 1], rsem_t.at[d], ypeer(lax.rem(col + d, 4))).start()
        pltpu.make_async_copy(topf.at[mine_t, my_rows], tops.at[mine_t, core, col, row], rsem_t.at[0]).start()
        for k, src in ((0, tlinv), (1, tuinv)):
            for d in (1, 2, 3):
                remote(src.at[mine_t, my_rows], tops.at[mine_t, core, 4 + k, row], ssem_v.at[k, d - 1], rsem_v.at[k, d], zpeer(d)).start()
            pltpu.make_async_copy(src.at[mine_t, my_rows], tops.at[mine_t, core, 4 + k, row], rsem_v.at[k, 0]).start()

    def collect_rows():
        for d in range(4):
            arrived(tops.at[0, 0, 0, 0], rsem_t.at[d])
        ref = tops.at[mine_t, core, pl.ds(0, 4), row]
        for d in (1, 2, 3):
            remote(ref, ref, ssem_v.at[2, d - 1], rsem_v.at[2, d], zpeer(d)).start()

    def share_top():
        for d in range(4):
            arrived(tops.at[0, 0, 0, 0], rsem_v.at[0, d])
            arrived(tops.at[0, 0, 0, 0], rsem_v.at[1, d])
        for d in (1, 2, 3):
            arrived(tops.at[0, 0, pl.ds(0, 4), 0], rsem_v.at[2, d])
        ref = tops.at[mine_t, core]
        for d in (1, 3, 2):
            remote(ref, ref, ssem_w.at[d - 1], rsem_w.at[d - 1], xpeer(d)).start()
        remote(ref, ref, ssem_p.at[0], rsem_p.at[0], partner).start()

    def hand_top(d):
        arrived(tops.at[0, 0], rsem_w.at[d - 1])
        ref = tops.at[lax.rem(mine_t + 4 - d, 4), core]
        remote(ref, ref, ssem_p.at[d], rsem_p.at[d], partner).start()

    def top_block(t, u):
        return jnp.concatenate([tops[t, h, u, r] for r in range(4) for h in range(2)], axis=0)

    def prepare_top():
        for d in range(4):
            arrived(tops.at[0, 0], rsem_p.at[d])
        for t in range(4):
            for u in range(4):
                if t != u:
                    blockh[4 * t + u], blockl[4 * t + u] = halves(top_block(t, u))
            for k in range(2):
                blockh[16 + 2 * t + k], blockl[16 + 2 * t + k] = halves(top_block(t, 4 + k).T)

    def top_product(b, k):
        return product((blockh[b], blockl[b]), (tsolh[k], tsoll[k]))

    def top_rhs_of(t):
        parts = []
        for r in range(4):
            for j in range(4):
                m = 4 * t + j
                parts.append(trhs[m % 2, r, (m // 8) * 4 + (m % 8) // 2])
        return jnp.concatenate(parts, axis=0)

    def solve_top():
        for t in range(4):
            value = top_rhs_of(t)
            for u in range(t):
                value = value - top_product(4 * t + u, u)
            value = product((blockh[16 + 2 * t], blockl[16 + 2 * t]), halves(value))
            tsol[t] = value
            tsolh[t], tsoll[t] = halves(value)
        for t in (3, 2, 1, 0):
            value = tsol[t]
            for u in range(3, t, -1):
                value = value - top_product(4 * t + u, u)
            value = product((blockh[17 + 2 * t], blockl[17 + 2 * t]), halves(value))
            tsol[t] = value
            tsolh[t], tsoll[t] = halves(value)

    def inverse_of(n):
        return linv.at[sub, n] if n < 8 else uinv.at[sub, 15 - n]

    def send_inverse(n):
        for d in (1, 2, 3):
            remote(inverse_of(n), inv.at[n, row], ssem_i.at[n, d - 1], rsem_i.at[n, d], zpeer(d)).start()
        pltpu.make_async_copy(inverse_of(n), inv.at[n, row], rsem_i.at[n, 0]).start()

    def prepare_inverse(n):
        for d in range(4):
            arrived(inv.at[0, 0], rsem_i.at[n, d])
        whole = inv[n].reshape(256, 256).T
        invh[n % 2], invl[n % 2] = halves(whole)

    def sub_block(i, k):
        return slab[k // 2, i, :, (k % 2) * 256 : (k % 2) * 256 + 256]

    def terms(n):
        if n < 8:
            return [(lambda k=k: sub_block(n, k), k) for k in range(n)]
        i = 15 - n
        return [(lambda k=k: sub_block(i, k), 15 - k) for k in range(7, i, -1)]

    def apply(block, n):
        return product(halves(block()), (solh[n], soll[n]))

    def base_of(n):
        if n < 8:
            return base[n]
        return sol[15 - n, rows] - coup[15 - n]

    def before(n):
        value = base_of(n)
        for block, k in terms(n):
            if k != n - 1:
                value = value - apply(block, k)
        return value

    def finish(n, value):
        for block, k in terms(n):
            if k == n - 1:
                value = value - apply(block, k)
        return value

    def start_gather(n, value):
        gath[n, rows] = value
        for d in (1, 2, 3):
            remote(gath.at[n, rows], gath.at[n, rows], ssem_g.at[n, d - 1], rsem_g.at[n, d - 1], zpeer(d)).start()

    def solve(n):
        for d in (1, 2, 3):
            arrived(gath.at[0, pl.ds(0, 64)], rsem_g.at[n, d - 1])
        value = product((invh[n % 2], invl[n % 2]), halves(gath[n]))
        sol[n] = value
        solh[n], soll[n] = halves(value)

    def mask(t):
        return present_ref[sub, t].astype(F32)

    def contrib(owner):
        pair = (
            jnp.concatenate([solh[2 * owner], solh[2 * owner + 1]], axis=0),
            jnp.concatenate([soll[2 * owner], soll[2 * owner + 1]], axis=0),
        )
        for t in range(4):
            value = product(halves(lowers[owner, t]), pair) * mask(t)
            part[pl.ds(4 * t, 4)] += value.reshape(4, 16, 128)

    def couple(first, last):
        total = None
        for t in range(4):
            value = product(halves(uppers[t, first:last].reshape((last - first) * 64, 256)), (tsolh[t], tsoll[t])) * mask(t)
            total = value if total is None else total + value
        return total.reshape(last - first, 64, 128)

    base_copy = pltpu.make_async_copy(
        rhs.at[sub, :, :, pl.ds(pl.multiple_of(half * 128, 128), 128)], base, misc.at[0]
    )
    base_copy.start()
    send_inverse(0)
    travel(first=True, sends=SEND_AT[-1])
    collect_top()
    send_inverse(1)
    quarter = lax.broadcasted_iota(jnp.int32, (256, 128), 1) // 32
    narrow = jnp.concatenate([toprhs[t].T for t in range(4)], axis=0)
    spread = jnp.concatenate([narrow] * 4, axis=1)
    here = jnp.where(jnp.logical_and(leaf // 4 == half, sub == 0), lax.rem(leaf, 4), -1)
    part[...] = -jnp.where(quarter == here, spread, 0.0).reshape(16, 16, 128)
    base_copy.wait()
    carried = base_of(0)

    for n in range(16):
        if n == 8:
            contrib(3)
            at("end")
            contrib(0)
            me = sub * 8 + leaf
            red[pl.ds(me, 1)] = part[pl.ds(me, 1)]
            for k, (o, d) in enumerate(group):
                peer, m = member(o, d)
                remote(part.at[m], red.at[me], ssem_r.at[k], rsem_r.at[k], peer).start()
            at("sum")
            hand_top(1)
            hand_top(3)
            for k in range(15):
                arrived(red.at[0], rsem_r.at[k])
            total = red[0]
            for m in range(1, 16):
                total = total + red[m]
            slot = sub * 4 + mine_t
            trhs[core, row, pl.ds(slot, 1)] = -total[None]
            ref = trhs.at[core, row, slot]
            for k, peer in enumerate(wide):
                remote(ref, ref, ssem_a.at[k], rsem_a.at[k], peer).start()
            hand_top(2)
            at("share")
            prepare_top()
            for k in range(31):
                arrived(red.at[0], rsem_a.at[k])
            remote(trhs.at[core], trhs.at[core], ssem_q.at[0], rsem_q.at[0], partner).start()
            arrived(trhs.at[0], rsem_q.at[0])
            solve_top()
            for o in range(4):

                @pl.when(col == o)
                def _():
                    remote(tsol.at[o ^ 1], swap, ssem_x.at[0], rsem_x.at[0], ypeer(o ^ 1)).start()

            at("top")
            value = sol[7, rows] - couple(7, 8)[0]
        else:
            value = finish(n, carried)
        start_gather(n, value)
        if n + 2 < 16:
            send_inverse(n + 2)
        travel(sends=SEND_AT.get(n, ()), relays=RELAY_AT.get(n, ()))
        prepare_inverse(n)
        if n == 0:
            collect_rows()
        if n == 1:
            share_top()
        travel(arrivals=ARRIVE_AT.get(n, ()))
        if n == 7:
            contrib(2)
        if n == 8:
            coup[0:7] = couple(0, 7)
        if n + 1 not in (8, 16):
            carried = before(n + 1)
        if n == 7:
            contrib(1)
        solve(n)
        if n >= 8:
            i = 15 - n
            o = i // 2
            place = sub_out.at[0, sub, i % 2, :, pl.ds(pl.multiple_of(half * 128, 128), 128)]

            @pl.when(col == o)
            def _():
                pltpu.make_async_copy(sol.at[n], place, rsem_o.at[i % 2, col]).start()

            @pl.when(col != o)
            def _():
                remote(sol.at[n], place, ssem_o.at[i], rsem_o.at[i % 2, col], ypeer(o)).start()

    arrived(swap, rsem_x.at[0])
    top = jnp.where(leaf // 4 == half, tsol[col], swap[...])
    q = lax.rem(leaf, 4)
    picked = top[:, 0:32]
    for k in range(1, 4):
        picked = jnp.where(q == k, top[:, 32 * k : 32 * k + 32], picked)
    top_out[0] = picked.T

    travel(last=True)
    for n in range(16):
        for d in range(3):
            arrived(inv.at[0, 0], ssem_i.at[n, d])
            arrived(gath.at[0, pl.ds(0, 64)], ssem_g.at[n, d])
    for k in range(15):
        arrived(red.at[0], ssem_r.at[k])
    for k in range(31):
        arrived(red.at[0], ssem_a.at[k])
    for d in range(3):
        arrived(tops.at[0, 0, 0, 0], ssem_t.at[d])
        arrived(tops.at[0, 0, 0, 0], ssem_v.at[0, d])
        arrived(tops.at[0, 0, 0, 0], ssem_v.at[1, d])
        arrived(tops.at[0, 0, pl.ds(0, 4), 0], ssem_v.at[2, d])
        arrived(tops.at[0, 0], ssem_w.at[d])
    for d in range(4):
        arrived(tops.at[0, 0], ssem_p.at[d])
    arrived(trhs.at[0], ssem_q.at[0])
    arrived(swap, ssem_x.at[0])
    for i in range(8):

        @pl.when(col != i // 2)
        def _():
            arrived(sol.at[0], ssem_o.at[i])

    for k in range(2):
        for c in range(4):
            arrived(sol.at[0], rsem_o.at[k, c])


def per_device(
    subtree_factor, sub_linv, sub_uinv, lower_panel, upper_panel, panel_rows, upper_level_factor, top_linv, top_uinv, sub_rhs, top_rhs
):
    anywhere = pl.BlockSpec(memory_space=pl.ANY)
    vmem = pl.BlockSpec(memory_space=pltpu.VMEM)
    dma = pltpu.SemaphoreType.DMA
    solved, top = pl.pallas_call(
        kernel,
        name="solve",
        out_shape=(
            jax.ShapeDtypeStruct((1, 2, 2, 256, 256), F32),
            jax.ShapeDtypeStruct((1, 32, 256), F32),
        ),
        in_specs=[pl.BlockSpec(memory_space=pltpu.SMEM)] + [anywhere] * 9 + [vmem],
        out_specs=(anywhere, vmem),
        scratch_shapes=[
            pltpu.VMEM((4, 8, 64, 512), F32),
            pltpu.VMEM((4, 4, 64, 512), F32),
            pltpu.VMEM((4, 8, 64, 256), F32),
            pltpu.VMEM((4, 2, 6, 4, 32, 256), F32),
            pltpu.VMEM((16, 4, 64, 256), F32),
            pltpu.VMEM((8, 64, 128), F32),
            pltpu.VMEM((16, 256, 128), F32),
            pltpu.VMEM((16, 256, 128), F32),
            pltpu.VMEM((16, 256, 128), BF16),
            pltpu.VMEM((16, 256, 128), BF16),
            pltpu.VMEM((2, 256, 256), BF16),
            pltpu.VMEM((2, 256, 256), BF16),
            pltpu.VMEM((8, 64, 128), F32),
            pltpu.VMEM((16, 16, 128), F32),
            pltpu.VMEM((16, 16, 128), F32),
            pltpu.VMEM((2, 4, 8, 16, 128), F32),
            pltpu.VMEM((256, 128), F32),
            pltpu.VMEM((24, 256, 256), BF16),
            pltpu.VMEM((24, 256, 256), BF16),
            pltpu.VMEM((4, 256, 128), F32),
            pltpu.VMEM((4, 256, 128), BF16),
            pltpu.VMEM((4, 256, 128), BF16),
            dma((NPOS, 3)),
            dma((NPOS, 4)),
            dma((16, 3)),
            dma((16, 4)),
            dma((16, 3)),
            dma((16, 3)),
            dma((15,)),
            dma((15,)),
            dma((31,)),
            dma((31,)),
            dma((8,)),
            dma((2, 4)),
            dma((1,)),
            dma((1,)),
            dma((1,)),
            dma((3,)),
            dma((4,)),
            dma((3, 3)),
            dma((3, 4)),
            dma((3,)),
            dma((3,)),
            dma((4,)),
            dma((4,)),
            dma((1,)),
            dma((1,)),
        ],
        compiler_params=pltpu.CompilerParams(collective_id=0, has_side_effects=True, vmem_limit_bytes=56 << 20),
    )(
        jnp.transpose(panel_rows[0]),
        subtree_factor[0],
        sub_linv[0],
        sub_uinv[0],
        lower_panel[0],
        upper_panel[0],
        upper_level_factor,
        top_linv,
        top_uinv,
        sub_rhs[0],
        jnp.swapaxes(top_rhs, 1, 2),
    )
    return solved, jnp.swapaxes(top, 1, 2)


def solution(mesh):
    placed = (
        P("leaf", None, None, "prow", "pcol"),
        P("leaf", None, None, "prow", None),
        P("leaf", None, None, "prow", None),
        P("leaf", None, "prow", None, "pcol"),
        P("leaf", None, None, "prow", "pcol"),
        P("leaf", None, None),
        P(None, "prow", "pcol"),
        P(None, "prow", None),
        P(None, "prow", None),
        P("leaf", None, None, "prow", None),
        P(None, "prow", "leaf"),
    )
    return jax.shard_map(
        per_device,
        mesh=mesh,
        in_specs=placed,
        out_specs=(P("leaf", None, "pcol", None, None), P("pcol", None, "leaf")),
        check_vma=False,
    )
```

```python
import jax
import jax.numpy as jnp
from jax import lax
from jax.experimental import pallas as pl
from jax.experimental.pallas import tpu as pltpu
from jax.sharding import PartitionSpec as P

MESH = pl.DeviceIdType.MESH
F32 = jnp.float32
BF16 = jnp.bfloat16
NPOS = 22
SEND_AT = {-1: (0, 1, 2), 0: (3,), 1: (4,), 2: (5,), 3: (6,), 4: (7, 8), 5: (9,), 6: (10,), 7: (11,), "sum": (12,), "share": (13, 14), "top": (15, 16), 8: (17, 18), 9: (19, 20), 10: (21,)}
RELAY_AT = {0: (0, 1), 1: (2,), 2: (3,), 3: (4,), 4: (5,), 5: (6, 7), 6: (8,), 7: (9, 10), "sum": (11,), "share": (12,), "top": (13, 14, 15), 8: (16, 17), 9: (18, 19), 10: (20, 21)}
ARRIVE_AT = {0: (0,), 1: (1,), 2: (2,), 3: (3,), 4: (4,), 5: (5,), 6: (6,), 7: (7, 8), "end": (9, 10), "ties": (11,), "top": (12, 13, 14, 15), 8: (16, 17), 9: (18, 19), 10: (20, 21)}


def halves(value):
    high = value.astype(BF16)
    return high, (value - high.astype(F32)).astype(BF16)


def product(left, right):
    def one(a, b):
        return jnp.dot(a, b, preferred_element_type=F32)

    return one(left[0], right[0]) + (one(left[0], right[1]) + one(left[1], right[0]))


def kernel(
    present_ref,
    factor,
    linv,
    uinv,
    lower,
    upper,
    topf,
    tlinv,
    tuinv,
    rhs,
    toprhs,
    sub_out,
    top_out,
    slab,
    lowers,
    uppers,
    tops,
    inv,
    base,
    gath,
    sol,
    solh,
    soll,
    invh,
    invl,
    coup,
    part,
    red,
    trhs,
    swap,
    blockh,
    blockl,
    ties,
    pairs,
    tsol,
    tsolh,
    tsoll,
    ssem_y,
    rsem_y,
    ssem_i,
    rsem_i,
    ssem_g,
    rsem_g,
    ssem_r,
    rsem_r,
    ssem_a,
    rsem_a,
    ssem_o,
    rsem_o,
    misc,
    ssem_x,
    rsem_x,
    ssem_t,
    rsem_t,
    ssem_v,
    rsem_v,
    ssem_w,
    rsem_w,
    ssem_p,
    rsem_p,
    ssem_q,
    rsem_q,
    ssem_e,
    rsem_e,
):
    leaf = lax.axis_index("leaf")
    row = lax.axis_index("prow")
    col = lax.axis_index("pcol")
    sub = col // 2
    half = lax.rem(col + sub, 2)
    beside = col + 1 - 2 * lax.rem(col, 2)
    across = 3 - col
    rows = pl.ds(pl.multiple_of(row * 64, 64), 64)

    def zpeer(d):
        return (leaf, lax.rem(row + d, 4), col)

    def ypeer(c):
        return (leaf, row, c)

    group = []
    for other in (0, 1):
        for d in range(8):
            if other or d:
                group.append((other, d))

    def member(other, d):
        there = lax.rem(leaf + d, 8)
        return (there, row, across if other else col), (1 - sub if other else sub) * 8 + there

    core = lax.rem(leaf, 2)
    mine_t = leaf // 2
    partner = (leaf + 1 - 2 * core, row, col)
    wide = []
    for other in (0, 1):
        for dx in range(4):
            for dr in range(4):
                if other or dx or dr:
                    wide.append((lax.rem(leaf + 2 * dx, 8), lax.rem(row + dr, 4), across if other else col))

    def xpeer(d):
        return (lax.rem(leaf + 2 * d, 8), row, col)

    barrier = pltpu.get_barrier_semaphore()
    greeted = wide + [ypeer(beside), ypeer(3 - beside)]
    greeted += [member(o, d)[0] for o, d in group if d % 2]
    for peer in greeted:
        pl.semaphore_signal(barrier, inc=1, device_id=peer, device_id_type=MESH)
    pl.semaphore_wait(barrier, len(greeted))

    def remote(src, dst, send, recv, peer):
        return pltpu.make_async_remote_copy(
            src_ref=src, dst_ref=dst, send_sem=send, recv_sem=recv, device_id=peer, device_id_type=MESH
        )

    def arrived(ref, sem):
        pltpu.make_async_copy(ref, ref, sem).wait()

    def piece(owner, p):
        near = 7 - 2 * owner
        if p < near:
            i = 2 * owner + 1 + p
            if p == 0:
                return lambda s: factor.at[s, i, :, pl.ds(0, 256)], slab.at[owner, i, :, pl.ds(0, 256)]
            return lambda s: factor.at[s, i], slab.at[owner, i]
        if p < near + 4:
            t = p - near
            return lambda s: lower.at[t, :, s], lowers.at[owner, t]
        if p < 11:
            return None
        if p == 11:
            return lambda s: factor.at[s, 2 * owner, :, pl.ds(256, 256)], ties.at[owner, row]
        if p < 16:
            i = pl.ds(2 * (p - 12), 2)
            return lambda s: upper.at[s, i], uppers.at[owner, i]
        i = 21 - p
        if i >= 2 * owner:
            return None
        return lambda s: factor.at[s, i], slab.at[owner, i]

    def travel(sends=(), relays=(), arrivals=(), first=False, last=False):
        for o in range(4):
            mine, there, over = o // 2, 1 - o // 2, 3 - o

            @pl.when(col == o)
            def _():
                if first:
                    for p in range(NPOS):
                        if piece(o, p):
                            src, dst = piece(o, p)
                            pltpu.make_async_copy(src(mine), dst, rsem_y.at[p, o]).start()
                for p in sends:
                    if piece(o, p):
                        src, dst = piece(o, p)
                        remote(src(mine), dst, ssem_y.at[p, 0], rsem_y.at[p, o], ypeer(o ^ 1)).start()
                        remote(src(there), dst, ssem_y.at[p, 1], rsem_y.at[p, o], ypeer(over)).start()
                for p in relays:
                    if piece(over, p):
                        dst = piece(over, p)[1]
                        arrived(dst, rsem_y.at[p, over])
                        remote(dst, dst, ssem_y.at[p, 2], rsem_y.at[p, over], ypeer(o ^ 1)).start()
                for p in arrivals:
                    for other in (o, o ^ 1, 3 - (o ^ 1)):
                        if piece(other, p):
                            arrived(piece(other, p)[1], rsem_y.at[p, other])
                if last:
                    for p in range(NPOS):
                        if piece(o, p):
                            dst = piece(o, p)[1]
                            arrived(dst, ssem_y.at[p, 0])
                            arrived(dst, ssem_y.at[p, 1])
                        if piece(over, p):
                            arrived(piece(over, p)[1], ssem_y.at[p, 2])

    def at(point):
        travel(SEND_AT.get(point, ()), RELAY_AT.get(point, ()), ARRIVE_AT.get(point, ()))

    my_rows = pl.ds(pl.multiple_of(core * 32, 32), 32)

    def collect_top():
        for d in (1, 2, 3):
            remote(topf.at[mine_t, my_rows], tops.at[mine_t, core, col, row], ssem_t.at[d - 1], rsem_t.at[d], ypeer(lax.rem(col + d, 4))).start()
        pltpu.make_async_copy(topf.at[mine_t, my_rows], tops.at[mine_t, core, col, row], rsem_t.at[0]).start()
        for k, src in ((0, tlinv), (1, tuinv)):
            for d in (1, 2, 3):
                remote(src.at[mine_t, my_rows], tops.at[mine_t, core, 4 + k, row], ssem_v.at[k, d - 1], rsem_v.at[k, d], zpeer(d)).start()
            pltpu.make_async_copy(src.at[mine_t, my_rows], tops.at[mine_t, core, 4 + k, row], rsem_v.at[k, 0]).start()

    def collect_rows():
        for d in range(4):
            arrived(tops.at[0, 0, 0, 0], rsem_t.at[d])
        ref = tops.at[mine_t, core, pl.ds(0, 4), row]
        for d in (1, 2, 3):
            remote(ref, ref, ssem_v.at[2, d - 1], rsem_v.at[2, d], zpeer(d)).start()

    def share_top():
        for d in range(4):
            arrived(tops.at[0, 0, 0, 0], rsem_v.at[0, d])
            arrived(tops.at[0, 0, 0, 0], rsem_v.at[1, d])
        for d in (1, 2, 3):
            arrived(tops.at[0, 0, pl.ds(0, 4), 0], rsem_v.at[2, d])
        ref = tops.at[mine_t, core]
        for d in (1, 3, 2):
            remote(ref, ref, ssem_w.at[d - 1], rsem_w.at[d - 1], xpeer(d)).start()
        remote(ref, ref, ssem_p.at[0], rsem_p.at[0], partner).start()

    def hand_top(d):
        arrived(tops.at[0, 0], rsem_w.at[d - 1])
        ref = tops.at[lax.rem(mine_t + 4 - d, 4), core]
        remote(ref, ref, ssem_p.at[d], rsem_p.at[d], partner).start()

    def top_block(t, u):
        return jnp.concatenate([tops[t, h, u, r] for r in range(4) for h in range(2)], axis=0)

    def prepare_top():
        for d in range(4):
            arrived(tops.at[0, 0], rsem_p.at[d])
        for t in range(4):
            for u in range(4):
                if t != u:
                    blockh[4 * t + u], blockl[4 * t + u] = halves(top_block(t, u))
            for k in range(2):
                blockh[16 + 2 * t + k], blockl[16 + 2 * t + k] = halves(top_block(t, 4 + k).T)

    def top_product(b, k):
        return product((blockh[b], blockl[b]), (tsolh[k], tsoll[k]))

    def top_rhs_of(t):
        parts = []
        for r in range(4):
            for j in range(4):
                m = 4 * t + j
                parts.append(trhs[m % 2, r, (m // 8) * 4 + (m % 8) // 2])
        return jnp.concatenate(parts, axis=0)

    def solve_top():
        for t in range(4):
            value = top_rhs_of(t)
            for u in range(t):
                value = value - top_product(4 * t + u, u)
            value = product((blockh[16 + 2 * t], blockl[16 + 2 * t]), halves(value))
            tsol[t] = value
            tsolh[t], tsoll[t] = halves(value)
        for t in (3, 2, 1, 0):
            value = tsol[t]
            for u in range(3, t, -1):
                value = value - top_product(4 * t + u, u)
            value = product((blockh[17 + 2 * t], blockl[17 + 2 * t]), halves(value))
            tsol[t] = value
            tsolh[t], tsoll[t] = halves(value)

    def inverse_of(n):
        return linv.at[sub, n] if n < 8 else uinv.at[sub, 15 - n]

    def send_inverse(n):
        for d in (1, 2, 3):
            remote(inverse_of(n), inv.at[n, row], ssem_i.at[n, d - 1], rsem_i.at[n, d], zpeer(d)).start()
        pltpu.make_async_copy(inverse_of(n), inv.at[n, row], rsem_i.at[n, 0]).start()

    def prepare_inverse(n):
        for d in range(4):
            arrived(inv.at[0, 0], rsem_i.at[n, d])
        invh[n], invl[n] = halves(inv[n].reshape(256, 256).T)

    def send_ties():
        ref = ties.at[:, row]
        for d in (1, 2, 3):
            remote(ref, ref, ssem_e.at[d - 1], rsem_e.at[d - 1], zpeer(d)).start()

    def sub_block(i, k):
        return slab[k // 2, i, :, (k % 2) * 256 : (k % 2) * 256 + 256]

    def terms(n):
        return [(lambda k=k: sub_block(n, k), k) for k in range(n)]

    def apply(block, n):
        return product(halves(block()), (solh[n], soll[n]))

    def base_of(n):
        return base[n]

    def pair_product(p, q):
        wide_block = slab[q, 2 * p : 2 * p + 2].reshape(128, 512)
        found = (
            jnp.concatenate([solh[8 + 2 * q], solh[9 + 2 * q]], axis=0),
            jnp.concatenate([soll[8 + 2 * q], soll[9 + 2 * q]], axis=0),
        )
        return product(halves(wide_block), found)

    def pair_base(p):
        value = jnp.concatenate([sol[2 * p, rows], sol[2 * p + 1, rows]], axis=0)
        return value - coup[2 * p : 2 * p + 2].reshape(128, 128)

    def start_pair(p, value):
        pairs[p, 0, rows] = value[:64]
        pairs[p, 1, rows] = value[64:]
        ref = pairs.at[p, :, rows]
        for d in (1, 2, 3):
            remote(ref, ref, ssem_g.at[8 + p, d - 1], rsem_g.at[8 + p, d - 1], zpeer(d)).start()

    def solve_pair(p):
        for d in (1, 2, 3):
            arrived(pairs.at[0, :, pl.ds(0, 64)], rsem_g.at[8 + p, d - 1])
        tie = halves(ties[p].reshape(256, 256))
        upper_n, lower_n = 15 - (2 * p + 1), 15 - 2 * p
        later = product((invh[upper_n], invl[upper_n]), halves(pairs[p, 1]))
        later_parts = halves(later)
        right = pairs[p, 0] - product(tie, later_parts)
        sooner = product((invh[lower_n], invl[lower_n]), halves(right))
        sol[9 + 2 * p] = later
        solh[9 + 2 * p], soll[9 + 2 * p] = later_parts
        sol[8 + 2 * p] = sooner
        solh[8 + 2 * p], soll[8 + 2 * p] = halves(sooner)

    def give_out(i):
        o = i // 2
        place = sub_out.at[0, sub, i % 2, :, pl.ds(pl.multiple_of(half * 128, 128), 128)]

        @pl.when(col == o)
        def _():
            pltpu.make_async_copy(sol.at[8 + i], place, rsem_o.at[i % 2, col]).start()

        @pl.when(col != o)
        def _():
            remote(sol.at[8 + i], place, ssem_o.at[i], rsem_o.at[i % 2, col], ypeer(o)).start()

    def before(n):
        value = base_of(n)
        for block, k in terms(n):
            if k != n - 1:
                value = value - apply(block, k)
        return value

    def finish(n, value):
        for block, k in terms(n):
            if k == n - 1:
                value = value - apply(block, k)
        return value

    def start_gather(n, value):
        gath[n, rows] = value
        for d in (1, 2, 3):
            remote(gath.at[n, rows], gath.at[n, rows], ssem_g.at[n, d - 1], rsem_g.at[n, d - 1], zpeer(d)).start()

    def solve(n):
        for d in (1, 2, 3):
            arrived(gath.at[0, pl.ds(0, 64)], rsem_g.at[n, d - 1])
        value = product((invh[n], invl[n]), halves(gath[n]))
        sol[n] = value
        solh[n], soll[n] = halves(value)

    def mask(t):
        return present_ref[sub, t].astype(F32)

    def contrib(owner):
        pair = (
            jnp.concatenate([solh[2 * owner], solh[2 * owner + 1]], axis=0),
            jnp.concatenate([soll[2 * owner], soll[2 * owner + 1]], axis=0),
        )
        for t in range(4):
            value = product(halves(lowers[owner, t]), pair) * mask(t)
            part[pl.ds(4 * t, 4)] += value.reshape(4, 16, 128)

    def couple(first, last):
        total = None
        for t in range(4):
            value = product(halves(uppers[t, first:last].reshape((last - first) * 64, 256)), (tsolh[t], tsoll[t])) * mask(t)
            total = value if total is None else total + value
        return total.reshape(last - first, 64, 128)

    base_copy = pltpu.make_async_copy(
        rhs.at[sub, :, :, pl.ds(pl.multiple_of(half * 128, 128), 128)], base, misc.at[0]
    )
    base_copy.start()
    send_inverse(0)
    travel(first=True, sends=SEND_AT[-1])
    collect_top()
    send_inverse(1)
    quarter = lax.broadcasted_iota(jnp.int32, (256, 128), 1) // 32
    narrow = jnp.concatenate([toprhs[t].T for t in range(4)], axis=0)
    spread = jnp.concatenate([narrow] * 4, axis=1)
    here = jnp.where(jnp.logical_and(leaf // 4 == half, sub == 0), lax.rem(leaf, 4), -1)
    part[...] = -jnp.where(quarter == here, spread, 0.0).reshape(16, 16, 128)
    base_copy.wait()
    carried = base_of(0)

    for n in range(8):
        start_gather(n, finish(n, carried))
        send_inverse(n + 2)
        travel(sends=SEND_AT.get(n, ()), relays=RELAY_AT.get(n, ()))
        prepare_inverse(n)
        if n == 0:
            collect_rows()
        if n == 1:
            share_top()
        travel(arrivals=ARRIVE_AT.get(n, ()))
        if n == 7:
            contrib(2)
        else:
            carried = before(n + 1)
        if n == 7:
            contrib(1)
        solve(n)

    contrib(3)
    at("end")
    contrib(0)
    me = sub * 8 + leaf
    red[pl.ds(me, 1)] = part[pl.ds(me, 1)]
    for k, (o, d) in enumerate(group):
        peer, m = member(o, d)
        remote(part.at[m], red.at[me], ssem_r.at[k], rsem_r.at[k], peer).start()
    at("sum")
    send_inverse(10)
    send_inverse(11)
    hand_top(1)
    hand_top(3)
    for k in range(15):
        arrived(red.at[0], rsem_r.at[k])
    total = red[0]
    for m in range(1, 16):
        total = total + red[m]
    slot = sub * 4 + mine_t
    trhs[core, row, pl.ds(slot, 1)] = -total[None]
    ref = trhs.at[core, row, slot]
    for k, peer in enumerate(wide):
        remote(ref, ref, ssem_a.at[k], rsem_a.at[k], peer).start()
    hand_top(2)
    at("share")
    send_inverse(12)
    send_inverse(13)
    prepare_top()
    prepare_inverse(8)
    prepare_inverse(9)
    at("ties")
    send_ties()
    for k in range(31):
        arrived(red.at[0], rsem_a.at[k])
    remote(trhs.at[core], trhs.at[core], ssem_q.at[0], rsem_q.at[0], partner).start()
    arrived(trhs.at[0], rsem_q.at[0])
    solve_top()
    for o in range(4):

        @pl.when(col == o)
        def _():
            remote(tsol.at[o ^ 1], swap, ssem_x.at[0], rsem_x.at[0], ypeer(o ^ 1)).start()

    send_inverse(14)
    send_inverse(15)
    at("top")

    coup[6:8] = couple(6, 8)
    carried = pair_base(3)
    for p in (3, 2, 1, 0):
        n = 11 - p
        value = carried
        if p < 3:
            value = value - pair_product(p, p + 1)
        start_pair(p, value)
        travel(sends=SEND_AT.get(n, ()), relays=RELAY_AT.get(n, ()))
        if p == 3:
            for d in range(3):
                arrived(ties.at[:, 0], rsem_e.at[d])
            coup[0:6] = couple(0, 6)
        else:
            give_out(2 * p + 3)
            give_out(2 * p + 2)
        if p:
            prepare_inverse(15 - (2 * p - 1))
            prepare_inverse(15 - (2 * p - 2))
            travel(arrivals=ARRIVE_AT.get(n, ()))
            carried = pair_base(p - 1)
            for q in range(3, p, -1):
                carried = carried - pair_product(p - 1, q)
        solve_pair(p)
    give_out(1)
    give_out(0)

    arrived(swap, rsem_x.at[0])
    top = jnp.where(leaf // 4 == half, tsol[col], swap[...])
    q = lax.rem(leaf, 4)
    picked = top[:, 0:32]
    for k in range(1, 4):
        picked = jnp.where(q == k, top[:, 32 * k : 32 * k + 32], picked)
    top_out[0] = picked.T

    travel(last=True)
    for n in range(16):
        for d in range(3):
            arrived(inv.at[0, 0], ssem_i.at[n, d])
    for n in range(8):
        for d in range(3):
            arrived(gath.at[0, pl.ds(0, 64)], ssem_g.at[n, d])
    for p in range(4):
        for d in range(3):
            arrived(pairs.at[0, :, pl.ds(0, 64)], ssem_g.at[8 + p, d])
    for d in range(3):
        arrived(ties.at[:, 0], ssem_e.at[d])
    for k in range(15):
        arrived(red.at[0], ssem_r.at[k])
    for k in range(31):
        arrived(red.at[0], ssem_a.at[k])
    for d in range(3):
        arrived(tops.at[0, 0, 0, 0], ssem_t.at[d])
        arrived(tops.at[0, 0, 0, 0], ssem_v.at[0, d])
        arrived(tops.at[0, 0, 0, 0], ssem_v.at[1, d])
        arrived(tops.at[0, 0, pl.ds(0, 4), 0], ssem_v.at[2, d])
        arrived(tops.at[0, 0], ssem_w.at[d])
    for d in range(4):
        arrived(tops.at[0, 0], ssem_p.at[d])
    arrived(trhs.at[0], ssem_q.at[0])
    arrived(swap, ssem_x.at[0])
    for i in range(8):

        @pl.when(col != i // 2)
        def _():
            arrived(sol.at[0], ssem_o.at[i])

    for k in range(2):
        for c in range(4):
            arrived(sol.at[0], rsem_o.at[k, c])


def per_device(
    subtree_factor, sub_linv, sub_uinv, lower_panel, upper_panel, panel_rows, upper_level_factor, top_linv, top_uinv, sub_rhs, top_rhs
):
    anywhere = pl.BlockSpec(memory_space=pl.ANY)
    vmem = pl.BlockSpec(memory_space=pltpu.VMEM)
    dma = pltpu.SemaphoreType.DMA
    solved, top = pl.pallas_call(
        kernel,
        name="solve",
        out_shape=(
            jax.ShapeDtypeStruct((1, 2, 2, 256, 256), F32),
            jax.ShapeDtypeStruct((1, 32, 256), F32),
        ),
        in_specs=[pl.BlockSpec(memory_space=pltpu.SMEM)] + [anywhere] * 9 + [vmem],
        out_specs=(anywhere, vmem),
        scratch_shapes=[
            pltpu.VMEM((4, 8, 64, 512), F32),
            pltpu.VMEM((4, 4, 64, 512), F32),
            pltpu.VMEM((4, 8, 64, 256), F32),
            pltpu.VMEM((4, 2, 6, 4, 32, 256), F32),
            pltpu.VMEM((16, 4, 64, 256), F32),
            pltpu.VMEM((8, 64, 128), F32),
            pltpu.VMEM((8, 256, 128), F32),
            pltpu.VMEM((16, 256, 128), F32),
            pltpu.VMEM((16, 256, 128), BF16),
            pltpu.VMEM((16, 256, 128), BF16),
            pltpu.VMEM((16, 256, 256), BF16),
            pltpu.VMEM((16, 256, 256), BF16),
            pltpu.VMEM((8, 64, 128), F32),
            pltpu.VMEM((16, 16, 128), F32),
            pltpu.VMEM((16, 16, 128), F32),
            pltpu.VMEM((2, 4, 8, 16, 128), F32),
            pltpu.VMEM((256, 128), F32),
            pltpu.VMEM((24, 256, 256), BF16),
            pltpu.VMEM((24, 256, 256), BF16),
            pltpu.VMEM((4, 4, 64, 256), F32),
            pltpu.VMEM((4, 2, 256, 128), F32),
            pltpu.VMEM((4, 256, 128), F32),
            pltpu.VMEM((4, 256, 128), BF16),
            pltpu.VMEM((4, 256, 128), BF16),
            dma((NPOS, 3)),
            dma((NPOS, 4)),
            dma((16, 3)),
            dma((16, 4)),
            dma((16, 3)),
            dma((16, 3)),
            dma((15,)),
            dma((15,)),
            dma((31,)),
            dma((31,)),
            dma((8,)),
            dma((2, 4)),
            dma((1,)),
            dma((1,)),
            dma((1,)),
            dma((3,)),
            dma((4,)),
            dma((3, 3)),
            dma((3, 4)),
            dma((3,)),
            dma((3,)),
            dma((4,)),
            dma((4,)),
            dma((1,)),
            dma((1,)),
            dma((3,)),
            dma((3,)),
        ],
        compiler_params=pltpu.CompilerParams(collective_id=0, has_side_effects=True, vmem_limit_bytes=56 << 20),
    )(
        jnp.transpose(panel_rows[0]),
        subtree_factor[0],
        sub_linv[0],
        sub_uinv[0],
        lower_panel[0],
        upper_panel[0],
        upper_level_factor,
        top_linv,
        top_uinv,
        sub_rhs[0],
        jnp.swapaxes(top_rhs, 1, 2),
    )
    return solved, jnp.swapaxes(top, 1, 2)


def solution(mesh):
    placed = (
        P("leaf", None, None, "prow", "pcol"),
        P("leaf", None, None, "prow", None),
        P("leaf", None, None, "prow", None),
        P("leaf", None, "prow", None, "pcol"),
        P("leaf", None, None, "prow", "pcol"),
        P("leaf", None, None),
        P(None, "prow", "pcol"),
        P(None, "prow", None),
        P(None, "prow", None),
        P("leaf", None, None, "prow", None),
        P(None, "prow", "leaf"),
    )
    return jax.shard_map(
        per_device,
        mesh=mesh,
        in_specs=placed,
        out_specs=(P("leaf", None, "pcol", None, None), P("pcol", None, "leaf")),
        check_vma=False,
    )
```

```python
import jax
import jax.numpy as jnp
from jax import lax
from jax.experimental import pallas as pl
from jax.experimental.pallas import tpu as pltpu
from jax.sharding import PartitionSpec as P

MESH = pl.DeviceIdType.MESH
F32 = jnp.float32
BF16 = jnp.bfloat16
NPOS = 22
OVER_AT = {-1: (0, 1, 2), 0: (3,), 1: (4,), 2: (5,), 3: (6, 7), 4: (8,), 5: (9, 10), 6: (11, 12, 13), 7: (14, 15), "share": (16, 17, 18), "top": (19, 20, 21)}
SEND_AT = {-1: (0, 1, 2), 0: (3,), 1: (4,), 2: (5,), 3: (6,), 4: (7, 8), 5: (9,), 6: (10,), 7: (11, 12), "sum": (13, 14), "share": (15,), "top": (16, 17, 18), 8: (19, 20, 21)}
RELAY_AT = {0: (0,), 1: (1, 2), 2: (3,), 3: (4,), 4: (5,), 5: (6, 7), 6: (8,), 7: (9, 10), "sum": (11, 12), "share": (13, 14, 15), 8: (16, 17, 18), 9: (19, 20, 21)}
ARRIVE_AT = {0: (0,), 1: (1,), 2: (2,), 3: (3,), 4: (4,), 5: (5,), 6: (6,), 7: (7, 8), "end": (9, 10), "ties": (11,), "top": (12, 13, 14, 15), 8: (16, 17), 9: (18, 19), 10: (20, 21)}


def halves(value):
    high = value.astype(BF16)
    return high, (value - high.astype(F32)).astype(BF16)


def product(left, right):
    def one(a, b):
        return jnp.dot(a, b, preferred_element_type=F32)

    return one(left[0], right[0]) + (one(left[0], right[1]) + one(left[1], right[0]))


def kernel(
    present_ref,
    factor,
    linv,
    uinv,
    lower,
    upper,
    topf,
    tlinv,
    tuinv,
    rhs,
    toprhs,
    sub_out,
    top_out,
    slab,
    lowers,
    uppers,
    tops,
    inv,
    base,
    gath,
    sol,
    solh,
    soll,
    invh,
    invl,
    coup,
    part,
    red,
    trhs,
    swap,
    blockh,
    blockl,
    ties,
    pairs,
    tsol,
    tsolh,
    tsoll,
    ssem_y,
    rsem_y,
    ssem_i,
    rsem_i,
    ssem_g,
    rsem_g,
    ssem_r,
    rsem_r,
    ssem_a,
    rsem_a,
    ssem_o,
    rsem_o,
    misc,
    ssem_x,
    rsem_x,
    ssem_t,
    rsem_t,
    ssem_v,
    rsem_v,
    ssem_w,
    rsem_w,
    ssem_p,
    rsem_p,
    ssem_q,
    rsem_q,
    ssem_e,
    rsem_e,
):
    leaf = lax.axis_index("leaf")
    row = lax.axis_index("prow")
    col = lax.axis_index("pcol")
    sub = col // 2
    half = lax.rem(col + sub, 2)
    beside = col + 1 - 2 * lax.rem(col, 2)
    across = 3 - col
    rows = pl.ds(pl.multiple_of(row * 64, 64), 64)

    def zpeer(d):
        return (leaf, lax.rem(row + d, 4), col)

    def ypeer(c):
        return (leaf, row, c)

    group = []
    for other in (0, 1):
        for d in range(8):
            if other or d:
                group.append((other, d))

    def member(other, d):
        there = lax.rem(leaf + d, 8)
        return (there, row, across if other else col), (1 - sub if other else sub) * 8 + there

    core = lax.rem(leaf, 2)
    mine_t = leaf // 2
    partner = (leaf + 1 - 2 * core, row, col)
    wide = []
    for other in (0, 1):
        for dx in range(4):
            for dr in range(4):
                if other or dx or dr:
                    wide.append((lax.rem(leaf + 2 * dx, 8), lax.rem(row + dr, 4), across if other else col))

    def xpeer(d):
        return (lax.rem(leaf + 2 * d, 8), row, col)

    barrier = pltpu.get_barrier_semaphore()
    greeted = wide + [ypeer(beside), ypeer(3 - beside)]
    greeted += [member(o, d)[0] for o, d in group if d % 2]
    for peer in greeted:
        pl.semaphore_signal(barrier, inc=1, device_id=peer, device_id_type=MESH)
    pl.semaphore_wait(barrier, len(greeted))

    def remote(src, dst, send, recv, peer):
        return pltpu.make_async_remote_copy(
            src_ref=src, dst_ref=dst, send_sem=send, recv_sem=recv, device_id=peer, device_id_type=MESH
        )

    def arrived(ref, sem):
        pltpu.make_async_copy(ref, ref, sem).wait()

    def piece(owner, p):
        near = 7 - 2 * owner
        if p < near:
            i = 2 * owner + 1 + p
            if p == 0:
                return lambda s: factor.at[s, i, :, pl.ds(0, 256)], slab.at[owner, i, :, pl.ds(0, 256)]
            return lambda s: factor.at[s, i], slab.at[owner, i]
        if p < near + 4:
            t = p - near
            return lambda s: lower.at[t, :, s], lowers.at[owner, t]
        if p < 11:
            return None
        if p == 11:
            return lambda s: factor.at[s, 2 * owner, :, pl.ds(256, 256)], ties.at[owner, row]
        if p < 16:
            i = pl.ds(2 * (p - 12), 2)
            return lambda s: upper.at[s, i], uppers.at[owner, i]
        i = 21 - p
        if i >= 2 * owner:
            return None
        return lambda s: factor.at[s, i], slab.at[owner, i]

    def travel(sends=(), relays=(), arrivals=(), overs=(), first=False, last=False):
        for o in range(4):
            mine, there, over = o // 2, 1 - o // 2, 3 - o

            @pl.when(col == o)
            def _():
                if first:
                    for p in range(NPOS):
                        if piece(o, p):
                            src, dst = piece(o, p)
                            pltpu.make_async_copy(src(mine), dst, rsem_y.at[p, o]).start()
                for p in overs:
                    if piece(o, p):
                        src, dst = piece(o, p)
                        remote(src(there), dst, ssem_y.at[p, 1], rsem_y.at[p, o], ypeer(over)).start()
                for p in relays:
                    if piece(over, p):
                        dst = piece(over, p)[1]
                        arrived(dst, rsem_y.at[p, over])
                        remote(dst, dst, ssem_y.at[p, 2], rsem_y.at[p, over], ypeer(o ^ 1)).start()
                for p in sends:
                    if piece(o, p):
                        src, dst = piece(o, p)
                        remote(src(mine), dst, ssem_y.at[p, 0], rsem_y.at[p, o], ypeer(o ^ 1)).start()
                for p in arrivals:
                    for other in (o, o ^ 1, 3 - (o ^ 1)):
                        if piece(other, p):
                            arrived(piece(other, p)[1], rsem_y.at[p, other])
                if last:
                    for p in range(NPOS):
                        if piece(o, p):
                            dst = piece(o, p)[1]
                            arrived(dst, ssem_y.at[p, 0])
                            arrived(dst, ssem_y.at[p, 1])
                        if piece(over, p):
                            arrived(piece(over, p)[1], ssem_y.at[p, 2])

    def at(point):
        travel(SEND_AT.get(point, ()), RELAY_AT.get(point, ()), ARRIVE_AT.get(point, ()), OVER_AT.get(point, ()))

    my_rows = pl.ds(pl.multiple_of(core * 32, 32), 32)

    def collect_top():
        for d in (1, 2, 3):
            remote(topf.at[mine_t, my_rows], tops.at[mine_t, core, col, row], ssem_t.at[d - 1], rsem_t.at[d], ypeer(lax.rem(col + d, 4))).start()
        pltpu.make_async_copy(topf.at[mine_t, my_rows], tops.at[mine_t, core, col, row], rsem_t.at[0]).start()
        for k, src in ((0, tlinv), (1, tuinv)):
            for d in (1, 2, 3):
                remote(src.at[mine_t, my_rows], tops.at[mine_t, core, 4 + k, row], ssem_v.at[k, d - 1], rsem_v.at[k, d], zpeer(d)).start()
            pltpu.make_async_copy(src.at[mine_t, my_rows], tops.at[mine_t, core, 4 + k, row], rsem_v.at[k, 0]).start()

    def collect_rows():
        for d in range(4):
            arrived(tops.at[0, 0, 0, 0], rsem_t.at[d])
        ref = tops.at[mine_t, core, pl.ds(0, 4), row]
        for d in (1, 2, 3):
            remote(ref, ref, ssem_v.at[2, d - 1], rsem_v.at[2, d], zpeer(d)).start()

    def share_top():
        for d in range(4):
            arrived(tops.at[0, 0, 0, 0], rsem_v.at[0, d])
            arrived(tops.at[0, 0, 0, 0], rsem_v.at[1, d])
        for d in (1, 2, 3):
            arrived(tops.at[0, 0, pl.ds(0, 4), 0], rsem_v.at[2, d])
        ref = tops.at[mine_t, core]
        for d in (1, 3, 2):
            remote(ref, ref, ssem_w.at[d - 1], rsem_w.at[d - 1], xpeer(d)).start()
        remote(ref, ref, ssem_p.at[0], rsem_p.at[0], partner).start()

    def hand_top(d):
        arrived(tops.at[0, 0], rsem_w.at[d - 1])
        ref = tops.at[lax.rem(mine_t + 4 - d, 4), core]
        remote(ref, ref, ssem_p.at[d], rsem_p.at[d], partner).start()

    def top_block(t, u):
        return jnp.concatenate([tops[t, h, u, r] for r in range(4) for h in range(2)], axis=0)

    def prepare_top():
        for d in range(4):
            arrived(tops.at[0, 0], rsem_p.at[d])
        for t in range(4):
            for u in range(4):
                if t != u:
                    blockh[4 * t + u], blockl[4 * t + u] = halves(top_block(t, u))
            for k in range(2):
                blockh[16 + 2 * t + k], blockl[16 + 2 * t + k] = halves(top_block(t, 4 + k).T)

    def top_product(b, k):
        return product((blockh[b], blockl[b]), (tsolh[k], tsoll[k]))

    def top_rhs_of(t):
        parts = []
        for r in range(4):
            for j in range(4):
                m = 4 * t + j
                parts.append(trhs[m % 2, r, (m // 8) * 4 + (m % 8) // 2])
        return jnp.concatenate(parts, axis=0)

    def solve_top():
        for t in range(4):
            value = top_rhs_of(t)
            for u in range(t):
                value = value - top_product(4 * t + u, u)
            value = product((blockh[16 + 2 * t], blockl[16 + 2 * t]), halves(value))
            tsol[t] = value
            tsolh[t], tsoll[t] = halves(value)
        for t in (3, 2, 1, 0):
            value = tsol[t]
            for u in range(3, t, -1):
                value = value - top_product(4 * t + u, u)
            value = product((blockh[17 + 2 * t], blockl[17 + 2 * t]), halves(value))
            tsol[t] = value
            tsolh[t], tsoll[t] = halves(value)

    def inverse_of(n):
        return linv.at[sub, n] if n < 8 else uinv.at[sub, 15 - n]

    def send_inverse(n):
        for d in (1, 2, 3):
            remote(inverse_of(n), inv.at[n, row], ssem_i.at[n, d - 1], rsem_i.at[n, d], zpeer(d)).start()
        pltpu.make_async_copy(inverse_of(n), inv.at[n, row], rsem_i.at[n, 0]).start()

    def prepare_inverse(n):
        for d in range(4):
            arrived(inv.at[0, 0], rsem_i.at[n, d])
        invh[n], invl[n] = halves(inv[n].reshape(256, 256).T)

    def send_tie(p):
        ref = ties.at[p, row]
        for d in (1, 2, 3):
            remote(ref, ref, ssem_e.at[p, d - 1], rsem_e.at[p, d - 1], zpeer(d)).start()

    def sub_block(i, k):
        return slab[k // 2, i, :, (k % 2) * 256 : (k % 2) * 256 + 256]

    def terms(n):
        return [(lambda k=k: sub_block(n, k), k) for k in range(n)]

    def apply(block, n):
        return product(halves(block()), (solh[n], soll[n]))

    def base_of(n):
        return base[n]

    def pair_product(p, q):
        wide_block = slab[q, 2 * p : 2 * p + 2].reshape(128, 512)
        found = (
            jnp.concatenate([solh[8 + 2 * q], solh[9 + 2 * q]], axis=0),
            jnp.concatenate([soll[8 + 2 * q], soll[9 + 2 * q]], axis=0),
        )
        return product(halves(wide_block), found)

    def pair_base(p):
        value = jnp.concatenate([sol[2 * p, rows], sol[2 * p + 1, rows]], axis=0)
        return value - coup[2 * p : 2 * p + 2].reshape(128, 128)

    def start_pair(p, value):
        pairs[p, 0, rows] = value[:64]
        pairs[p, 1, rows] = value[64:]
        ref = pairs.at[p, :, rows]
        for d in (1, 2, 3):
            remote(ref, ref, ssem_g.at[8 + p, d - 1], rsem_g.at[8 + p, d - 1], zpeer(d)).start()

    def solve_pair(p):
        for d in (1, 2, 3):
            arrived(pairs.at[0, :, pl.ds(0, 64)], rsem_g.at[8 + p, d - 1])
        for d in range(3):
            arrived(ties.at[0, 0], rsem_e.at[p, d])
        tie = halves(ties[p].reshape(256, 256))
        upper_n, lower_n = 15 - (2 * p + 1), 15 - 2 * p
        later = product((invh[upper_n], invl[upper_n]), halves(pairs[p, 1]))
        later_parts = halves(later)
        right = pairs[p, 0] - product(tie, later_parts)
        sooner = product((invh[lower_n], invl[lower_n]), halves(right))
        sol[9 + 2 * p] = later
        solh[9 + 2 * p], soll[9 + 2 * p] = later_parts
        sol[8 + 2 * p] = sooner
        solh[8 + 2 * p], soll[8 + 2 * p] = halves(sooner)

    def give_out(i):
        o = i // 2
        place = sub_out.at[0, sub, i % 2, :, pl.ds(pl.multiple_of(half * 128, 128), 128)]

        @pl.when(col == o)
        def _():
            pltpu.make_async_copy(sol.at[8 + i], place, rsem_o.at[i % 2, col]).start()

        @pl.when(col != o)
        def _():
            remote(sol.at[8 + i], place, ssem_o.at[i], rsem_o.at[i % 2, col], ypeer(o)).start()

    def before(n):
        value = base_of(n)
        for block, k in terms(n):
            if k != n - 1:
                value = value - apply(block, k)
        return value

    def finish(n, value):
        for block, k in terms(n):
            if k == n - 1:
                value = value - apply(block, k)
        return value

    def start_gather(n, value):
        gath[n, rows] = value
        for d in (1, 2, 3):
            remote(gath.at[n, rows], gath.at[n, rows], ssem_g.at[n, d - 1], rsem_g.at[n, d - 1], zpeer(d)).start()

    def solve(n):
        for d in (1, 2, 3):
            arrived(gath.at[0, pl.ds(0, 64)], rsem_g.at[n, d - 1])
        value = product((invh[n], invl[n]), halves(gath[n]))
        sol[n] = value
        solh[n], soll[n] = halves(value)

    def mask(t):
        return present_ref[sub, t].astype(F32)

    def contrib(owner):
        pair = (
            jnp.concatenate([solh[2 * owner], solh[2 * owner + 1]], axis=0),
            jnp.concatenate([soll[2 * owner], soll[2 * owner + 1]], axis=0),
        )
        for t in range(4):
            value = product(halves(lowers[owner, t]), pair) * mask(t)
            part[pl.ds(4 * t, 4)] += value.reshape(4, 16, 128)

    def couple(first, last):
        total = None
        for t in range(4):
            value = product(halves(uppers[t, first:last].reshape((last - first) * 64, 256)), (tsolh[t], tsoll[t])) * mask(t)
            total = value if total is None else total + value
        return total.reshape(last - first, 64, 128)

    base_copy = pltpu.make_async_copy(
        rhs.at[sub, :, :, pl.ds(pl.multiple_of(half * 128, 128), 128)], base, misc.at[0]
    )
    base_copy.start()
    travel(overs=OVER_AT[-1][:1], sends=SEND_AT[-1][:1])
    base_copy.wait()
    start_gather(0, base_of(0))
    send_inverse(0)
    travel(overs=OVER_AT[-1][1:], sends=SEND_AT[-1][1:], first=True)
    collect_top()
    send_inverse(1)
    quarter = lax.broadcasted_iota(jnp.int32, (256, 128), 1) // 32
    narrow = jnp.concatenate([toprhs[t].T for t in range(4)], axis=0)
    spread = jnp.concatenate([narrow] * 4, axis=1)
    here = jnp.where(jnp.logical_and(leaf // 4 == half, sub == 0), lax.rem(leaf, 4), -1)
    part[...] = -jnp.where(quarter == here, spread, 0.0).reshape(16, 16, 128)
    carried = None

    for n in range(8):
        if n:
            start_gather(n, finish(n, carried))
        send_inverse(n + 2)
        travel(sends=SEND_AT.get(n, ()), relays=RELAY_AT.get(n, ()), overs=OVER_AT.get(n, ()))
        prepare_inverse(n)
        if n == 2:
            collect_rows()
        if n == 3:
            share_top()
        travel(arrivals=ARRIVE_AT.get(n, ()))
        if n == 7:
            contrib(2)
        else:
            carried = before(n + 1)
        if n == 7:
            contrib(1)
        solve(n)

    contrib(3)
    at("end")
    contrib(0)
    me = sub * 8 + leaf
    red[pl.ds(me, 1)] = part[pl.ds(me, 1)]
    for k, (o, d) in enumerate(group):
        peer, m = member(o, d)
        remote(part.at[m], red.at[me], ssem_r.at[k], rsem_r.at[k], peer).start()
    at("sum")
    send_inverse(10)
    hand_top(1)
    hand_top(3)
    for k in range(15):
        arrived(red.at[0], rsem_r.at[k])
    total = red[0]
    for m in range(1, 16):
        total = total + red[m]
    slot = sub * 4 + mine_t
    trhs[core, row, pl.ds(slot, 1)] = -total[None]
    ref = trhs.at[core, row, slot]
    for k, peer in enumerate(wide):
        remote(ref, ref, ssem_a.at[k], rsem_a.at[k], peer).start()
    hand_top(2)
    at("share")
    send_inverse(11)
    at("ties")
    send_tie(3)
    send_inverse(12)
    prepare_top()
    prepare_inverse(8)
    prepare_inverse(9)
    for k in range(31):
        arrived(red.at[0], rsem_a.at[k])
    remote(trhs.at[core], trhs.at[core], ssem_q.at[0], rsem_q.at[0], partner).start()
    arrived(trhs.at[0], rsem_q.at[0])
    send_inverse(13)
    solve_top()
    for o in range(4):

        @pl.when(col == o)
        def _():
            remote(tsol.at[o ^ 1], swap, ssem_x.at[0], rsem_x.at[0], ypeer(o ^ 1)).start()

    at("top")

    coup[6:8] = couple(6, 8)
    carried = pair_base(3)
    for p in (3, 2, 1, 0):
        n = 11 - p
        value = carried
        if p < 3:
            value = value - pair_product(p, p + 1)
        start_pair(p, value)
        if p:
            send_tie(p - 1)
        if p > 1:
            send_inverse(17 - p)
        travel(sends=SEND_AT.get(n, ()), relays=RELAY_AT.get(n, ()), overs=OVER_AT.get(n, ()))
        if p == 3:
            coup[0:6] = couple(0, 6)
        else:
            give_out(2 * p + 3)
            give_out(2 * p + 2)
        if p:
            prepare_inverse(15 - (2 * p - 1))
            prepare_inverse(15 - (2 * p - 2))
            travel(arrivals=ARRIVE_AT.get(n, ()))
            carried = pair_base(p - 1)
            for q in range(3, p, -1):
                carried = carried - pair_product(p - 1, q)
        solve_pair(p)
    give_out(1)
    give_out(0)

    arrived(swap, rsem_x.at[0])
    top = jnp.where(leaf // 4 == half, tsol[col], swap[...])
    q = lax.rem(leaf, 4)
    picked = top[:, 0:32]
    for k in range(1, 4):
        picked = jnp.where(q == k, top[:, 32 * k : 32 * k + 32], picked)
    top_out[0] = picked.T

    travel(last=True)
    for n in range(16):
        for d in range(3):
            arrived(inv.at[0, 0], ssem_i.at[n, d])
    for n in range(8):
        for d in range(3):
            arrived(gath.at[0, pl.ds(0, 64)], ssem_g.at[n, d])
    for p in range(4):
        for d in range(3):
            arrived(pairs.at[0, :, pl.ds(0, 64)], ssem_g.at[8 + p, d])
    for p in range(4):
        for d in range(3):
            arrived(ties.at[0, 0], ssem_e.at[p, d])
    for k in range(15):
        arrived(red.at[0], ssem_r.at[k])
    for k in range(31):
        arrived(red.at[0], ssem_a.at[k])
    for d in range(3):
        arrived(tops.at[0, 0, 0, 0], ssem_t.at[d])
        arrived(tops.at[0, 0, 0, 0], ssem_v.at[0, d])
        arrived(tops.at[0, 0, 0, 0], ssem_v.at[1, d])
        arrived(tops.at[0, 0, pl.ds(0, 4), 0], ssem_v.at[2, d])
        arrived(tops.at[0, 0], ssem_w.at[d])
    for d in range(4):
        arrived(tops.at[0, 0], ssem_p.at[d])
    arrived(trhs.at[0], ssem_q.at[0])
    arrived(swap, ssem_x.at[0])
    for i in range(8):

        @pl.when(col != i // 2)
        def _():
            arrived(sol.at[0], ssem_o.at[i])

    for k in range(2):
        for c in range(4):
            arrived(sol.at[0], rsem_o.at[k, c])


def per_device(
    subtree_factor, sub_linv, sub_uinv, lower_panel, upper_panel, panel_rows, upper_level_factor, top_linv, top_uinv, sub_rhs, top_rhs
):
    anywhere = pl.BlockSpec(memory_space=pl.ANY)
    vmem = pl.BlockSpec(memory_space=pltpu.VMEM)
    dma = pltpu.SemaphoreType.DMA
    solved, top = pl.pallas_call(
        kernel,
        name="solve",
        out_shape=(
            jax.ShapeDtypeStruct((1, 2, 2, 256, 256), F32),
            jax.ShapeDtypeStruct((1, 32, 256), F32),
        ),
        in_specs=[pl.BlockSpec(memory_space=pltpu.SMEM)] + [anywhere] * 9 + [vmem],
        out_specs=(anywhere, vmem),
        scratch_shapes=[
            pltpu.VMEM((4, 8, 64, 512), F32),
            pltpu.VMEM((4, 4, 64, 512), F32),
            pltpu.VMEM((4, 8, 64, 256), F32),
            pltpu.VMEM((4, 2, 6, 4, 32, 256), F32),
            pltpu.VMEM((16, 4, 64, 256), F32),
            pltpu.VMEM((8, 64, 128), F32),
            pltpu.VMEM((8, 256, 128), F32),
            pltpu.VMEM((16, 256, 128), F32),
            pltpu.VMEM((16, 256, 128), BF16),
            pltpu.VMEM((16, 256, 128), BF16),
            pltpu.VMEM((16, 256, 256), BF16),
            pltpu.VMEM((16, 256, 256), BF16),
            pltpu.VMEM((8, 64, 128), F32),
            pltpu.VMEM((16, 16, 128), F32),
            pltpu.VMEM((16, 16, 128), F32),
            pltpu.VMEM((2, 4, 8, 16, 128), F32),
            pltpu.VMEM((256, 128), F32),
            pltpu.VMEM((24, 256, 256), BF16),
            pltpu.VMEM((24, 256, 256), BF16),
            pltpu.VMEM((4, 4, 64, 256), F32),
            pltpu.VMEM((4, 2, 256, 128), F32),
            pltpu.VMEM((4, 256, 128), F32),
            pltpu.VMEM((4, 256, 128), BF16),
            pltpu.VMEM((4, 256, 128), BF16),
            dma((NPOS, 3)),
            dma((NPOS, 4)),
            dma((16, 3)),
            dma((16, 4)),
            dma((16, 3)),
            dma((16, 3)),
            dma((15,)),
            dma((15,)),
            dma((31,)),
            dma((31,)),
            dma((8,)),
            dma((2, 4)),
            dma((1,)),
            dma((1,)),
            dma((1,)),
            dma((3,)),
            dma((4,)),
            dma((3, 3)),
            dma((3, 4)),
            dma((3,)),
            dma((3,)),
            dma((4,)),
            dma((4,)),
            dma((1,)),
            dma((1,)),
            dma((4, 3)),
            dma((4, 3)),
        ],
        compiler_params=pltpu.CompilerParams(collective_id=0, has_side_effects=True, vmem_limit_bytes=56 << 20),
    )(
        jnp.transpose(panel_rows[0]),
        subtree_factor[0],
        sub_linv[0],
        sub_uinv[0],
        lower_panel[0],
        upper_panel[0],
        upper_level_factor,
        top_linv,
        top_uinv,
        sub_rhs[0],
        jnp.swapaxes(top_rhs, 1, 2),
    )
    return solved, jnp.swapaxes(top, 1, 2)


def solution(mesh):
    placed = (
        P("leaf", None, None, "prow", "pcol"),
        P("leaf", None, None, "prow", None),
        P("leaf", None, None, "prow", None),
        P("leaf", None, "prow", None, "pcol"),
        P("leaf", None, None, "prow", "pcol"),
        P("leaf", None, None),
        P(None, "prow", "pcol"),
        P(None, "prow", None),
        P(None, "prow", None),
        P("leaf", None, None, "prow", None),
        P(None, "prow", "leaf"),
    )
    return jax.shard_map(
        per_device,
        mesh=mesh,
        in_specs=placed,
        out_specs=(P("leaf", None, "pcol", None, None), P("pcol", None, "leaf")),
        check_vma=False,
    )
```

```python
import jax
import jax.numpy as jnp
from jax import lax
from jax.experimental import pallas as pl
from jax.experimental.pallas import tpu as pltpu
from jax.sharding import PartitionSpec as P

MESH = pl.DeviceIdType.MESH
F32 = jnp.float32
BF16 = jnp.bfloat16
NPOS = 22
OVER_AT = {-1: (0, 1, 2), 0: (3,), 1: (4,), 2: (5,), 3: (6, 7), 4: (8,), 5: (9, 10), 6: (11, 12, 13), 7: (14, 15), "share": (16, 17, 18), "top": (19, 20, 21)}
SEND_AT = {-1: (0, 1, 2), 0: (3,), 1: (4,), 2: (5,), 3: (6,), 4: (7, 8), 5: (9,), 6: (10,), 7: (11, 12), "sum": (13, 14), "share": (15,), "top": (16, 17, 18), 8: (19, 20, 21)}
RELAY_AT = {0: (0,), 1: (1, 2), 2: (3,), 3: (4,), 4: (5,), 5: (6, 7), 6: (8,), 7: (9, 10), "sum": (11, 12), "share": (13, 14, 15), 8: (16, 17, 18), 9: (19, 20, 21)}
ARRIVE_AT = {0: (0,), 1: (1,), 2: (2,), 3: (3,), 4: (4,), 5: (5,), 6: (6,), 7: (7, 8), "end": (9, 10), "ties": (11,), "top": (12, 13, 14, 15), 8: (16, 17), 9: (18, 19), 10: (20, 21)}


def halves(value):
    high = value.astype(BF16)
    return high, (value - high.astype(F32)).astype(BF16)


def product(left, right):
    def one(a, b):
        return jnp.dot(a, b, preferred_element_type=F32)

    return one(left[0], right[0]) + (one(left[0], right[1]) + one(left[1], right[0]))


def kernel(
    present_ref,
    factor,
    linv,
    uinv,
    lower,
    upper,
    topf,
    tlinv,
    tuinv,
    rhs,
    toprhs,
    sub_out,
    top_out,
    slab,
    lowers,
    uppers,
    tops,
    inv,
    base,
    gath,
    sol,
    solh,
    soll,
    invh,
    invl,
    coup,
    part,
    red,
    trhs,
    swap,
    blockh,
    blockl,
    ties,
    pairs,
    tsol,
    tsolh,
    tsoll,
    ssem_y,
    rsem_y,
    ssem_i,
    rsem_i,
    ssem_g,
    rsem_g,
    ssem_r,
    rsem_r,
    ssem_a,
    rsem_a,
    ssem_o,
    rsem_o,
    misc,
    ssem_x,
    rsem_x,
    ssem_t,
    rsem_t,
    ssem_v,
    rsem_v,
    ssem_w,
    rsem_w,
    ssem_p,
    rsem_p,
    ssem_q,
    rsem_q,
    ssem_e,
    rsem_e,
    ssem_h,
    rsem_h,
):
    leaf = lax.axis_index("leaf")
    row = lax.axis_index("prow")
    col = lax.axis_index("pcol")
    sub = col // 2
    half = lax.rem(col + sub, 2)
    beside = col + 1 - 2 * lax.rem(col, 2)
    across = 3 - col
    rows = pl.ds(pl.multiple_of(row * 64, 64), 64)

    def zpeer(d):
        return (leaf, lax.rem(row + d, 4), col)

    def ypeer(c):
        return (leaf, row, c)

    group = []
    for other in (0, 1):
        for d in range(8):
            if other or d:
                group.append((other, d))

    def member(other, d):
        there = lax.rem(leaf + d, 8)
        return (there, row, across if other else col), (1 - sub if other else sub) * 8 + there

    core = lax.rem(leaf, 2)
    mine_t = leaf // 2
    partner = (leaf + 1 - 2 * core, row, col)
    wide = []
    for other in (0, 1):
        for dx in range(4):
            for dr in range(4):
                if other or dx or dr:
                    wide.append((lax.rem(leaf + 2 * dx, 8), lax.rem(row + dr, 4), across if other else col))

    def xpeer(d):
        return (lax.rem(leaf + 2 * d, 8), row, col)

    barrier = pltpu.get_barrier_semaphore()
    greeted = wide + [ypeer(beside), ypeer(3 - beside)]
    greeted += [member(o, d)[0] for o, d in group if d % 2]
    for peer in greeted:
        pl.semaphore_signal(barrier, inc=1, device_id=peer, device_id_type=MESH)
    pl.semaphore_wait(barrier, len(greeted))

    def remote(src, dst, send, recv, peer):
        return pltpu.make_async_remote_copy(
            src_ref=src, dst_ref=dst, send_sem=send, recv_sem=recv, device_id=peer, device_id_type=MESH
        )

    def arrived(ref, sem):
        pltpu.make_async_copy(ref, ref, sem).wait()

    def piece(owner, p):
        near = 7 - 2 * owner
        if p < near:
            i = 2 * owner + 1 + p
            if p == 0:
                return lambda s: factor.at[s, i, :, pl.ds(0, 256)], slab.at[owner, i, :, pl.ds(0, 256)]
            return lambda s: factor.at[s, i], slab.at[owner, i]
        if p < near + 4:
            t = p - near
            return lambda s: lower.at[t, :, s], lowers.at[owner, t]
        if p < 11:
            return None
        if p == 11:
            return lambda s: factor.at[s, 2 * owner, :, pl.ds(256, 256)], ties.at[owner, row]
        if p < 16:
            i = pl.ds(2 * (p - 12), 2)
            return lambda s: upper.at[s, i], uppers.at[owner, i]
        i = 21 - p
        if i >= 2 * owner:
            return None
        return lambda s: factor.at[s, i], slab.at[owner, i]

    def travel(sends=(), relays=(), arrivals=(), overs=(), first=False, last=False):
        for o in range(4):
            mine, there, over = o // 2, 1 - o // 2, 3 - o

            @pl.when(col == o)
            def _():
                if first:
                    for p in range(NPOS):
                        if piece(o, p):
                            src, dst = piece(o, p)
                            pltpu.make_async_copy(src(mine), dst, rsem_y.at[p, o]).start()
                for p in overs:
                    if piece(o, p):
                        src, dst = piece(o, p)
                        remote(src(there), dst, ssem_y.at[p, 1], rsem_y.at[p, o], ypeer(over)).start()
                for p in relays:
                    if piece(over, p):
                        dst = piece(over, p)[1]
                        arrived(dst, rsem_y.at[p, over])
                        remote(dst, dst, ssem_y.at[p, 2], rsem_y.at[p, over], ypeer(o ^ 1)).start()
                for p in sends:
                    if piece(o, p):
                        src, dst = piece(o, p)
                        remote(src(mine), dst, ssem_y.at[p, 0], rsem_y.at[p, o], ypeer(o ^ 1)).start()
                for p in arrivals:
                    for other in (o, o ^ 1, 3 - (o ^ 1)):
                        if piece(other, p):
                            arrived(piece(other, p)[1], rsem_y.at[p, other])
                if last:
                    for p in range(NPOS):
                        if piece(o, p):
                            dst = piece(o, p)[1]
                            arrived(dst, ssem_y.at[p, 0])
                            arrived(dst, ssem_y.at[p, 1])
                        if piece(over, p):
                            arrived(piece(over, p)[1], ssem_y.at[p, 2])

    def at(point):
        travel(SEND_AT.get(point, ()), RELAY_AT.get(point, ()), ARRIVE_AT.get(point, ()), OVER_AT.get(point, ()))

    my_rows = pl.ds(pl.multiple_of(core * 32, 32), 32)

    def collect_top():
        for d in (1, 2, 3):
            remote(topf.at[mine_t, my_rows], tops.at[mine_t, core, col, row], ssem_t.at[d - 1], rsem_t.at[d], ypeer(lax.rem(col + d, 4))).start()
        pltpu.make_async_copy(topf.at[mine_t, my_rows], tops.at[mine_t, core, col, row], rsem_t.at[0]).start()
        for k, src in ((0, tlinv), (1, tuinv)):
            for d in (1, 2, 3):
                remote(src.at[mine_t, my_rows], tops.at[mine_t, core, 4 + k, row], ssem_v.at[k, d - 1], rsem_v.at[k, d], zpeer(d)).start()
            pltpu.make_async_copy(src.at[mine_t, my_rows], tops.at[mine_t, core, 4 + k, row], rsem_v.at[k, 0]).start()

    def collect_rows():
        for d in range(4):
            arrived(tops.at[0, 0, 0, 0], rsem_t.at[d])
        ref = tops.at[mine_t, core, pl.ds(0, 4), row]
        for d in (1, 2, 3):
            remote(ref, ref, ssem_v.at[2, d - 1], rsem_v.at[2, d], zpeer(d)).start()

    def share_top():
        for d in range(4):
            arrived(tops.at[0, 0, 0, 0], rsem_v.at[0, d])
            arrived(tops.at[0, 0, 0, 0], rsem_v.at[1, d])
        for d in (1, 2, 3):
            arrived(tops.at[0, 0, pl.ds(0, 4), 0], rsem_v.at[2, d])
        for j in range(1, 4):
            ref = tops.at[mine_t, core, lax.rem(mine_t + j, 4)]
            for d in (1, 3, 2):
                remote(ref, ref, ssem_w.at[j, d - 1], rsem_w.at[j, d - 1], xpeer(d)).start()
        ref = tops.at[mine_t, core, pl.ds(4, 2)]
        for d in (1, 3, 2):
            remote(ref, ref, ssem_w.at[0, d - 1], rsem_w.at[0, d - 1], xpeer(d)).start()
        ref = tops.at[mine_t, core]
        remote(ref, ref, ssem_p.at[0], rsem_p.at[0], partner).start()

    def hand_top(d):
        arrived(tops.at[0, 0, pl.ds(0, 2)], rsem_w.at[0, d - 1])
        for j in range(1, 4):
            arrived(tops.at[0, 0, 0], rsem_w.at[j, d - 1])
        there = lax.rem(mine_t + 4 - d, 4)
        for j in range(1, 4):
            ref = tops.at[there, core, lax.rem(there + j, 4)]
            remote(ref, ref, ssem_h.at[j, d - 1], rsem_h.at[j, d - 1], partner).start()
        ref = tops.at[there, core, pl.ds(4, 2)]
        remote(ref, ref, ssem_h.at[0, d - 1], rsem_h.at[0, d - 1], partner).start()

    def top_block(t, u):
        return jnp.concatenate([tops[t, h, u, r] for r in range(4) for h in range(2)], axis=0)

    def prepare_top():
        arrived(tops.at[0, 0], rsem_p.at[0])
        for d in range(3):
            arrived(tops.at[0, 0, pl.ds(0, 2)], rsem_h.at[0, d])
            for j in range(1, 4):
                arrived(tops.at[0, 0, 0], rsem_h.at[j, d])
        for t in range(4):
            for u in range(4):
                if t != u:
                    blockh[4 * t + u], blockl[4 * t + u] = halves(top_block(t, u))
            for k in range(2):
                blockh[16 + 2 * t + k], blockl[16 + 2 * t + k] = halves(top_block(t, 4 + k).T)

    def top_product(b, k):
        return product((blockh[b], blockl[b]), (tsolh[k], tsoll[k]))

    def top_rhs_of(t):
        parts = []
        for r in range(4):
            for j in range(4):
                m = 4 * t + j
                parts.append(trhs[m % 2, r, (m // 8) * 4 + (m % 8) // 2])
        return jnp.concatenate(parts, axis=0)

    def solve_top():
        for t in range(4):
            value = top_rhs_of(t)
            for u in range(t):
                value = value - top_product(4 * t + u, u)
            value = product((blockh[16 + 2 * t], blockl[16 + 2 * t]), halves(value))
            tsol[t] = value
            tsolh[t], tsoll[t] = halves(value)
        for t in (3, 2, 1, 0):
            value = tsol[t]
            for u in range(3, t, -1):
                value = value - top_product(4 * t + u, u)
            value = product((blockh[17 + 2 * t], blockl[17 + 2 * t]), halves(value))
            tsol[t] = value
            tsolh[t], tsoll[t] = halves(value)

    def inverse_of(n):
        return linv.at[sub, n] if n < 8 else uinv.at[sub, 15 - n]

    def send_inverse(n):
        for d in (1, 2, 3):
            remote(inverse_of(n), inv.at[n, row], ssem_i.at[n, d - 1], rsem_i.at[n, d], zpeer(d)).start()
        pltpu.make_async_copy(inverse_of(n), inv.at[n, row], rsem_i.at[n, 0]).start()

    def prepare_inverse(n):
        for d in range(4):
            arrived(inv.at[0, 0], rsem_i.at[n, d])
        invh[n], invl[n] = halves(inv[n].reshape(256, 256).T)

    def send_tie(p):
        ref = ties.at[p, row]
        for d in (1, 2, 3):
            remote(ref, ref, ssem_e.at[p, d - 1], rsem_e.at[p, d - 1], zpeer(d)).start()

    def sub_block(i, k):
        return slab[k // 2, i, :, (k % 2) * 256 : (k % 2) * 256 + 256]

    def terms(n):
        return [(lambda k=k: sub_block(n, k), k) for k in range(n)]

    def apply(block, n):
        return product(halves(block()), (solh[n], soll[n]))

    def base_of(n):
        return base[n]

    def pair_product(p, q):
        wide_block = slab[q, 2 * p : 2 * p + 2].reshape(128, 512)
        found = (
            jnp.concatenate([solh[8 + 2 * q], solh[9 + 2 * q]], axis=0),
            jnp.concatenate([soll[8 + 2 * q], soll[9 + 2 * q]], axis=0),
        )
        return product(halves(wide_block), found)

    def pair_base(p):
        value = jnp.concatenate([sol[2 * p, rows], sol[2 * p + 1, rows]], axis=0)
        return value - coup[2 * p : 2 * p + 2].reshape(128, 128)

    def start_pair(p, value):
        pairs[p, 0, rows] = value[:64]
        pairs[p, 1, rows] = value[64:]
        ref = pairs.at[p, :, rows]
        for d in (1, 2, 3):
            remote(ref, ref, ssem_g.at[8 + p, d - 1], rsem_g.at[8 + p, d - 1], zpeer(d)).start()

    def solve_pair(p):
        for d in (1, 2, 3):
            arrived(pairs.at[0, :, pl.ds(0, 64)], rsem_g.at[8 + p, d - 1])
        for d in range(3):
            arrived(ties.at[0, 0], rsem_e.at[p, d])
        tie = halves(ties[p].reshape(256, 256))
        upper_n, lower_n = 15 - (2 * p + 1), 15 - 2 * p
        later = product((invh[upper_n], invl[upper_n]), halves(pairs[p, 1]))
        later_parts = halves(later)
        right = pairs[p, 0] - product(tie, later_parts)
        sooner = product((invh[lower_n], invl[lower_n]), halves(right))
        sol[9 + 2 * p] = later
        solh[9 + 2 * p], soll[9 + 2 * p] = later_parts
        sol[8 + 2 * p] = sooner
        solh[8 + 2 * p], soll[8 + 2 * p] = halves(sooner)

    def give_out(i):
        o = i // 2
        place = sub_out.at[0, sub, i % 2, :, pl.ds(pl.multiple_of(half * 128, 128), 128)]

        @pl.when(col == o)
        def _():
            pltpu.make_async_copy(sol.at[8 + i], place, rsem_o.at[i % 2, col]).start()

        @pl.when(col != o)
        def _():
            remote(sol.at[8 + i], place, ssem_o.at[i], rsem_o.at[i % 2, col], ypeer(o)).start()

    def before(n):
        value = base_of(n)
        for block, k in terms(n):
            if k != n - 1:
                value = value - apply(block, k)
        return value

    def finish(n, value):
        for block, k in terms(n):
            if k == n - 1:
                value = value - apply(block, k)
        return value

    def start_gather(n, value):
        gath[n, rows] = value
        for d in (1, 2, 3):
            remote(gath.at[n, rows], gath.at[n, rows], ssem_g.at[n, d - 1], rsem_g.at[n, d - 1], zpeer(d)).start()

    def solve(n):
        for d in (1, 2, 3):
            arrived(gath.at[0, pl.ds(0, 64)], rsem_g.at[n, d - 1])
        value = product((invh[n], invl[n]), halves(gath[n]))
        sol[n] = value
        solh[n], soll[n] = halves(value)

    def mask(t):
        return present_ref[sub, t].astype(F32)

    def contrib(owner):
        pair = (
            jnp.concatenate([solh[2 * owner], solh[2 * owner + 1]], axis=0),
            jnp.concatenate([soll[2 * owner], soll[2 * owner + 1]], axis=0),
        )
        for t in range(4):
            value = product(halves(lowers[owner, t]), pair) * mask(t)
            part[pl.ds(4 * t, 4)] += value.reshape(4, 16, 128)

    def couple(first, last):
        total = None
        for t in range(4):
            value = product(halves(uppers[t, first:last].reshape((last - first) * 64, 256)), (tsolh[t], tsoll[t])) * mask(t)
            total = value if total is None else total + value
        return total.reshape(last - first, 64, 128)

    base_copy = pltpu.make_async_copy(
        rhs.at[sub, :, :, pl.ds(pl.multiple_of(half * 128, 128), 128)], base, misc.at[0]
    )
    base_copy.start()
    travel(overs=OVER_AT[-1][:1], sends=SEND_AT[-1][:1])
    base_copy.wait()
    start_gather(0, base_of(0))
    send_inverse(0)
    travel(overs=OVER_AT[-1][1:], sends=SEND_AT[-1][1:], first=True)
    collect_top()
    send_inverse(1)
    quarter = lax.broadcasted_iota(jnp.int32, (256, 128), 1) // 32
    narrow = jnp.concatenate([toprhs[t].T for t in range(4)], axis=0)
    spread = jnp.concatenate([narrow] * 4, axis=1)
    here = jnp.where(jnp.logical_and(leaf // 4 == half, sub == 0), lax.rem(leaf, 4), -1)
    part[...] = -jnp.where(quarter == here, spread, 0.0).reshape(16, 16, 128)
    carried = None

    for n in range(8):
        if n:
            start_gather(n, finish(n, carried))
        send_inverse(n + 2)
        travel(sends=SEND_AT.get(n, ()), relays=RELAY_AT.get(n, ()), overs=OVER_AT.get(n, ()))
        prepare_inverse(n)
        if n == 1:
            collect_rows()
        if n == 2:
            share_top()
        travel(arrivals=ARRIVE_AT.get(n, ()))
        if n == 7:
            contrib(2)
        else:
            carried = before(n + 1)
        if n == 7:
            contrib(1)
        solve(n)

    contrib(3)
    at("end")
    contrib(0)
    me = sub * 8 + leaf
    red[pl.ds(me, 1)] = part[pl.ds(me, 1)]
    for k, (o, d) in enumerate(group):
        peer, m = member(o, d)
        remote(part.at[m], red.at[me], ssem_r.at[k], rsem_r.at[k], peer).start()
    at("sum")
    send_inverse(10)
    hand_top(1)
    hand_top(3)
    for k in range(15):
        arrived(red.at[0], rsem_r.at[k])
    total = red[0]
    for m in range(1, 16):
        total = total + red[m]
    slot = sub * 4 + mine_t
    trhs[core, row, pl.ds(slot, 1)] = -total[None]
    ref = trhs.at[core, row, slot]
    for k, peer in enumerate(wide):
        remote(ref, ref, ssem_a.at[k], rsem_a.at[k], peer).start()
    hand_top(2)
    at("share")
    send_inverse(11)
    at("ties")
    send_tie(3)
    send_inverse(12)
    prepare_top()
    prepare_inverse(8)
    prepare_inverse(9)
    for k in range(31):
        arrived(red.at[0], rsem_a.at[k])
    remote(trhs.at[core], trhs.at[core], ssem_q.at[0], rsem_q.at[0], partner).start()
    arrived(trhs.at[0], rsem_q.at[0])
    send_inverse(13)
    solve_top()
    for o in range(4):

        @pl.when(col == o)
        def _():
            remote(tsol.at[o ^ 1], swap, ssem_x.at[0], rsem_x.at[0], ypeer(o ^ 1)).start()

    at("top")

    coup[6:8] = couple(6, 8)
    carried = pair_base(3)
    for p in (3, 2, 1, 0):
        n = 11 - p
        value = carried
        if p < 3:
            value = value - pair_product(p, p + 1)
        start_pair(p, value)
        if p:
            send_tie(p - 1)
        if p > 1:
            send_inverse(17 - p)
        travel(sends=SEND_AT.get(n, ()), relays=RELAY_AT.get(n, ()), overs=OVER_AT.get(n, ()))
        if p == 3:
            coup[0:6] = couple(0, 6)
        else:
            give_out(2 * p + 3)
            give_out(2 * p + 2)
        if p:
            prepare_inverse(15 - (2 * p - 1))
            prepare_inverse(15 - (2 * p - 2))
            travel(arrivals=ARRIVE_AT.get(n, ()))
            carried = pair_base(p - 1)
            for q in range(3, p, -1):
                carried = carried - pair_product(p - 1, q)
        solve_pair(p)
    give_out(1)
    give_out(0)

    arrived(swap, rsem_x.at[0])
    top = jnp.where(leaf // 4 == half, tsol[col], swap[...])
    q = lax.rem(leaf, 4)
    picked = top[:, 0:32]
    for k in range(1, 4):
        picked = jnp.where(q == k, top[:, 32 * k : 32 * k + 32], picked)
    top_out[0] = picked.T

    travel(last=True)
    for n in range(16):
        for d in range(3):
            arrived(inv.at[0, 0], ssem_i.at[n, d])
    for n in range(8):
        for d in range(3):
            arrived(gath.at[0, pl.ds(0, 64)], ssem_g.at[n, d])
    for p in range(4):
        for d in range(3):
            arrived(pairs.at[0, :, pl.ds(0, 64)], ssem_g.at[8 + p, d])
    for p in range(4):
        for d in range(3):
            arrived(ties.at[0, 0], ssem_e.at[p, d])
    for k in range(15):
        arrived(red.at[0], ssem_r.at[k])
    for k in range(31):
        arrived(red.at[0], ssem_a.at[k])
    for d in range(3):
        arrived(tops.at[0, 0, 0, 0], ssem_t.at[d])
        arrived(tops.at[0, 0, 0, 0], ssem_v.at[0, d])
        arrived(tops.at[0, 0, 0, 0], ssem_v.at[1, d])
        arrived(tops.at[0, 0, pl.ds(0, 4), 0], ssem_v.at[2, d])
        for sem in (ssem_w, ssem_h):
            arrived(tops.at[0, 0, pl.ds(0, 2)], sem.at[0, d])
            for j in range(1, 4):
                arrived(tops.at[0, 0, 0], sem.at[j, d])
    arrived(tops.at[0, 0], ssem_p.at[0])
    arrived(trhs.at[0], ssem_q.at[0])
    arrived(swap, ssem_x.at[0])
    for i in range(8):

        @pl.when(col != i // 2)
        def _():
            arrived(sol.at[0], ssem_o.at[i])

    for k in range(2):
        for c in range(4):
            arrived(sol.at[0], rsem_o.at[k, c])


def per_device(
    subtree_factor, sub_linv, sub_uinv, lower_panel, upper_panel, panel_rows, upper_level_factor, top_linv, top_uinv, sub_rhs, top_rhs
):
    anywhere = pl.BlockSpec(memory_space=pl.ANY)
    vmem = pl.BlockSpec(memory_space=pltpu.VMEM)
    dma = pltpu.SemaphoreType.DMA
    solved, top = pl.pallas_call(
        kernel,
        name="solve",
        out_shape=(
            jax.ShapeDtypeStruct((1, 2, 2, 256, 256), F32),
            jax.ShapeDtypeStruct((1, 32, 256), F32),
        ),
        in_specs=[pl.BlockSpec(memory_space=pltpu.SMEM)] + [anywhere] * 9 + [vmem],
        out_specs=(anywhere, vmem),
        scratch_shapes=[
            pltpu.VMEM((4, 8, 64, 512), F32),
            pltpu.VMEM((4, 4, 64, 512), F32),
            pltpu.VMEM((4, 8, 64, 256), F32),
            pltpu.VMEM((4, 2, 6, 4, 32, 256), F32),
            pltpu.VMEM((16, 4, 64, 256), F32),
            pltpu.VMEM((8, 64, 128), F32),
            pltpu.VMEM((8, 256, 128), F32),
            pltpu.VMEM((16, 256, 128), F32),
            pltpu.VMEM((16, 256, 128), BF16),
            pltpu.VMEM((16, 256, 128), BF16),
            pltpu.VMEM((16, 256, 256), BF16),
            pltpu.VMEM((16, 256, 256), BF16),
            pltpu.VMEM((8, 64, 128), F32),
            pltpu.VMEM((16, 16, 128), F32),
            pltpu.VMEM((16, 16, 128), F32),
            pltpu.VMEM((2, 4, 8, 16, 128), F32),
            pltpu.VMEM((256, 128), F32),
            pltpu.VMEM((24, 256, 256), BF16),
            pltpu.VMEM((24, 256, 256), BF16),
            pltpu.VMEM((4, 4, 64, 256), F32),
            pltpu.VMEM((4, 2, 256, 128), F32),
            pltpu.VMEM((4, 256, 128), F32),
            pltpu.VMEM((4, 256, 128), BF16),
            pltpu.VMEM((4, 256, 128), BF16),
            dma((NPOS, 3)),
            dma((NPOS, 4)),
            dma((16, 3)),
            dma((16, 4)),
            dma((16, 3)),
            dma((16, 3)),
            dma((15,)),
            dma((15,)),
            dma((31,)),
            dma((31,)),
            dma((8,)),
            dma((2, 4)),
            dma((1,)),
            dma((1,)),
            dma((1,)),
            dma((3,)),
            dma((4,)),
            dma((3, 3)),
            dma((3, 4)),
            dma((4, 3)),
            dma((4, 3)),
            dma((1,)),
            dma((1,)),
            dma((1,)),
            dma((1,)),
            dma((4, 3)),
            dma((4, 3)),
            dma((4, 3)),
            dma((4, 3)),
        ],
        compiler_params=pltpu.CompilerParams(collective_id=0, has_side_effects=True, vmem_limit_bytes=56 << 20),
    )(
        jnp.transpose(panel_rows[0]),
        subtree_factor[0],
        sub_linv[0],
        sub_uinv[0],
        lower_panel[0],
        upper_panel[0],
        upper_level_factor,
        top_linv,
        top_uinv,
        sub_rhs[0],
        jnp.swapaxes(top_rhs, 1, 2),
    )
    return solved, jnp.swapaxes(top, 1, 2)


def solution(mesh):
    placed = (
        P("leaf", None, None, "prow", "pcol"),
        P("leaf", None, None, "prow", None),
        P("leaf", None, None, "prow", None),
        P("leaf", None, "prow", None, "pcol"),
        P("leaf", None, None, "prow", "pcol"),
        P("leaf", None, None),
        P(None, "prow", "pcol"),
        P(None, "prow", None),
        P(None, "prow", None),
        P("leaf", None, None, "prow", None),
        P(None, "prow", "leaf"),
    )
    return jax.shard_map(
        per_device,
        mesh=mesh,
        in_specs=placed,
        out_specs=(P("leaf", None, "pcol", None, None), P("pcol", None, "leaf")),
        check_vma=False,
    )
```
